128 devices in a mesh: gx: 4 (over x), gy: 32 (over z, y, core).
Axes of the slice: x: 4, y: 4, z: 4, core: 2. Of those that a mesh axis runs over, the one named last changes fastest.
Arguments:
- densities: bfloat16 [16, 524288], P(None, ('gx', 'gy')), may hold values from -6 to 6
- points: float32 [3, 524288], P(None, ('gx', 'gy')), may hold values from 0 to 1
- weights: float32 [524288], P(('gx', 'gy')), may hold values from 0.03 to 0.6
- near_offsets: int32 [4096, 13], P(('gx', 'gy')), may hold values from -8 to 8, as said below
- leaf_basis: bfloat16 [4096, 64, 128], P(('gx', 'gy')), may hold values from -0.5 to 0.5
- transfer: bfloat16 [4096, 64, 64], P(('gx', 'gy')), may hold values from -0.75 to 0.75
- send_lists: int32 [128, 17, 16], P(('gx', 'gy')), may hold values from 0 to 31
- relay_refs: int32 [4096, 32], P(('gx', 'gy')), may hold values from 0 to 271, as said below
- leaf_coupling: bfloat16 [4096, 32, 64, 64], P(('gx', 'gy')), may hold values from -0.25 to 0.25
- coarse_refs: int32 [512, 32], P(('gx', 'gy')), may hold values from 0 to 511
- coarse_coupling: bfloat16 [512, 32, 64, 64], P(('gx', 'gy')), may hold values from -0.125 to 0.125
Outputs:
- potential: float32 [16, 524288], P(None, ('gx', 'gy'))
The draws below stay inside these ranges and needn't reach their ends.
Inputs may be any that keep to these rules, and one draw needn't show every extreme that they name: `near_offsets`: each leaf's offsets are distinct and the first is 0; a partner outside the leaves contributes nothing. `relay_refs`: a value never names an owner l // 32 + value // 16 - 8 outside 0 to 127; within the rows of each device's 32 leaves every other value is used at least once.
All inputs are finite; a program needn't handle non-finite values.
Results may differ from the reference program's by a relative error of at most 0.0065.
Values may be sent and summed in bfloat16 or wider, within the bound.
No kernel may reach another device: no remote copies, remote signals or barrier semaphores. Data moves between devices by JAX's collectives and lax.ppermute only.
A program may use at most 128 MiB of HBM per device.

```python
import math
import jax
import jax.numpy as jnp
from jax import lax

RHS = 16
RANK = 64
LEAF_PTS = 128
LEAF_DEV = 32
NEAR = 13
REACH = 8
WINDOW = 8
FAR0 = 32
FAR1 = 32
LEAVES = 4096
POINTS = 524288
CLUSTERS = 512
CAPACITY = 16
N_GX = 4
N_GY = 32


def draw_near_offsets(key, part):

    def one_leaf(leaf_key):
        order = jax.random.permutation(leaf_key, 2 * REACH)
        picked = order[:NEAR - 1]
        shifted = jnp.where(picked < REACH, picked - REACH, picked - REACH + 1)
        return jnp.concatenate([jnp.zeros((1,), jnp.int32), shifted.astype(jnp.int32)])
    return jax.vmap(one_leaf)(jax.random.split(key, LEAVES)).astype(jnp.int32)


def draw_relay_refs(key, part):
    device_count = LEAVES // LEAF_DEV
    slot_total = (2 * WINDOW + 1) * CAPACITY
    total = LEAF_DEV * FAR0

    def one_device(device_index, device_key):
        bits_key, sign_key, slot_key, order_key = jax.random.split(device_key, 4)
        bits = jax.random.randint(bits_key, (total,), 0, 2 ** WINDOW)
        magnitude = jnp.zeros((total,), jnp.int32)
        for level in range(1, WINDOW + 1):
            magnitude = magnitude + (bits < 2 ** (WINDOW - level)).astype(jnp.int32)
        sign = jax.random.randint(sign_key, (total,), 0, 2) * 2 - 1
        offset = magnitude * sign
        owner = device_index + offset
        inside = (owner >= 0) & (owner < device_count)
        offset = jnp.where(inside, offset, -offset)
        slot = jax.random.randint(slot_key, (total,), 0, CAPACITY)
        extra = (offset + WINDOW) * CAPACITY + slot
        positions = jnp.arange(total, dtype=jnp.int32)
        cover = jnp.minimum(positions, slot_total - 1)
        cover_owner = device_index + cover // CAPACITY - WINDOW
        cover_fine = (positions < slot_total) & (cover_owner >= 0) & (cover_owner < device_count)
        mixed = jnp.where(cover_fine, cover, extra)
        return jax.random.permutation(order_key, mixed)
    blocks = jax.vmap(one_device)(jnp.arange(device_count, dtype=jnp.int32), jax.random.split(key, device_count))
    return blocks.reshape(LEAVES, FAR0).astype(jnp.int32)


def set_ends(entries, own_key, low, largest):
    longest = entries.shape.index(max(entries.shape))
    spots = []
    for shift in (0, 1):
        where = [jax.random.randint(jax.random.fold_in(own_key, axis), (), 0, length) for axis, length in enumerate(entries.shape)]
        where[longest] = (where[longest] + shift) % entries.shape[longest]
        spots.append(tuple(where))
    return entries.at[spots[0]].set(low).at[spots[1]].set(largest)


def block_scale(rng, extent, cuts, least, top_value):
    def one(position, shards_of):
        draws = jax.random.uniform(jax.random.fold_in(jax.random.fold_in(rng, 6), position), (shards_of,), jnp.float32, least / len(cuts), top_value / len(cuts))
        return jnp.repeat(jnp.exp(draws), extent[position] // shards_of).reshape((-1,) + (1,) * (len(extent) - position - 1))

    loudness = one(*cuts[0])
    for cut in cuts[1:]:
        loudness = loudness * one(*cut)
    return loudness


def normal_values(key, shape, spread, limit, cuts=(), kind=jnp.bfloat16):
    values = spread * jax.random.normal(key, shape, jnp.float32)
    if cuts:
        values = values * block_scale(key, shape, cuts, -0.22, 0.18)
    return jnp.clip(values, -limit, limit).astype(kind)


def setup_inputs(seed: int = 0) -> dict:
    streams_of = jax.random.split(jax.random.key(seed), 12)
    return {
        "densities": normal_values(streams_of[0], (RHS, POINTS), 1.0, 6.0, ((1, 128),)),
        "points": jnp.clip(1.0 * jax.random.uniform(streams_of[1], (3, POINTS), jnp.float32) ** block_scale(streams_of[1], (3, POINTS), ((1, 128),), -0.2, 0.2), 0.0, 1.0),
        "weights": jnp.clip(jnp.exp(math.log(0.6) - 2.9957323 * jax.random.uniform(streams_of[2], (POINTS,), jnp.float32) ** block_scale(streams_of[2], (POINTS,), ((0, 128),), -0.2, 0.2)), 0.03, 0.6),
        "near_offsets": draw_near_offsets(jax.random.fold_in(streams_of[11], 71), 0),
        "leaf_basis": normal_values(streams_of[4], (LEAVES, RANK, LEAF_PTS), LEAF_PTS ** -0.5, 0.5, ((0, 128),)),
        "transfer": normal_values(streams_of[5], (LEAVES, RANK, RANK), RANK ** -0.5, 0.75, ((0, 128),)),
        "send_lists": set_ends(jax.random.randint(streams_of[6], (N_GX * N_GY, 2 * WINDOW + 1, CAPACITY), 0, LEAF_DEV), jax.random.fold_in(streams_of[6], 1), 0, LEAF_DEV - 1).astype(jnp.int32),
        "relay_refs": draw_relay_refs(jax.random.fold_in(streams_of[11], 71), 0),
        "leaf_coupling": normal_values(streams_of[8], (LEAVES, FAR0, RANK, RANK), (RANK * FAR0 // 4) ** -0.5, 0.25, ((0, 128),)),
        "coarse_refs": set_ends(jax.random.randint(streams_of[9], (CLUSTERS, FAR1), 0, CLUSTERS), jax.random.fold_in(streams_of[9], 1), 0, CLUSTERS - 1).astype(jnp.int32),
        "coarse_coupling": normal_values(streams_of[10], (CLUSTERS, FAR1, RANK, RANK), (RANK * FAR1) ** -0.5, 0.125, ((0, 128),)),
    }


core_square = 0.0004
four_pi = 4.0 * math.pi

def near_field(densities, points, weights, near_offsets):
    rim_cells = REACH * LEAF_PTS
    packed = jnp.concatenate([densities.astype(jnp.float32), points, weights[None, :]], axis=0)
    padded = jnp.pad(packed, ((0, 0), (rim_cells, rim_cells)))
    extended = padded.reshape(RHS + 4, LEAVES + 2 * REACH, LEAF_PTS)
    row_points = points.reshape(3, LEAVES, LEAF_PTS)
    partners = (jnp.arange(LEAVES, dtype=jnp.int32)[:, None] + REACH + near_offsets).astype(jnp.int32)

    def near_block(block_index):
        partner_rows = lax.dynamic_slice_in_dim(partners, block_index * 8, 8, 0)
        partner_data = jnp.take(extended, partner_rows, axis=1)
        own_points = lax.dynamic_slice_in_dim(row_points, block_index * 8, 8, 1)
        distance = jnp.zeros((8, LEAF_PTS, NEAR, LEAF_PTS), jnp.float32)
        for component in range(3):
            offset_part = own_points[component][:, :, None, None] - partner_data[RHS + component][:, None, :, :]
            distance = distance + offset_part * offset_part
        kernel = (partner_data[RHS + 3][:, None, :, :] / (four_pi * jnp.sqrt(distance + core_square))).astype(jnp.bfloat16)
        partner_values = partner_data[:RHS].astype(jnp.bfloat16)
        return jnp.einsum('lisj,rlsj->rli', kernel.astype(jnp.float32), partner_values.astype(jnp.float32))
    blocks_out = lax.map(near_block, jnp.arange(LEAVES // 8, dtype=jnp.int32))
    return jnp.transpose(blocks_out, (1, 0, 2, 3)).reshape(RHS, POINTS)

def reference(densities, points, weights, near_offsets, leaf_basis, transfer, send_lists, relay_refs, leaf_coupling, coarse_refs, coarse_coupling):
    values = densities.astype(jnp.float32).reshape(RHS, LEAVES, LEAF_PTS)
    basis_wide = leaf_basis.astype(jnp.float32)
    coeff0 = jnp.einsum('lkm,rlm->lrk', basis_wide, values).astype(jnp.bfloat16)
    device_count = LEAVES // LEAF_DEV

    def relay_block(device_index):
        refs_block = lax.dynamic_slice_in_dim(relay_refs, device_index * LEAF_DEV, LEAF_DEV, 0)
        window_index = (refs_block // CAPACITY).astype(jnp.int32)
        slot_index = (refs_block % CAPACITY).astype(jnp.int32)
        source = jnp.clip(device_index + window_index - WINDOW, 0, device_count - 1).astype(jnp.int32)
        chosen = send_lists[source, 2 * WINDOW - window_index, slot_index]
        column = (source * LEAF_DEV + chosen).astype(jnp.int32)
        picked = jnp.take(coeff0, column, axis=0).astype(jnp.float32)
        coupling = lax.dynamic_slice_in_dim(leaf_coupling, device_index * LEAF_DEV, LEAF_DEV, 0).astype(jnp.float32)
        return jnp.einsum('lsab,lsrb->lra', coupling, picked)
    local0 = lax.map(relay_block, jnp.arange(device_count, dtype=jnp.int32)).reshape(LEAVES, RHS, RANK)
    transfer_wide = transfer.astype(jnp.float32).reshape(CLUSTERS, 8, RANK, RANK)
    coeff1 = jnp.einsum('qcab,qcra->qrb', transfer_wide, coeff0.astype(jnp.float32).reshape(CLUSTERS, 8, RHS, RANK)).astype(jnp.bfloat16)
    coarse_picked = jnp.take(coeff1, coarse_refs, axis=0).astype(jnp.float32)
    local1 = jnp.einsum('qsab,qsrb->qra', coarse_coupling.astype(jnp.float32), coarse_picked).astype(jnp.bfloat16)
    downward = jnp.einsum('qcab,qrb->qcra', transfer_wide, local1.astype(jnp.float32)).reshape(LEAVES, RHS, RANK)
    leaf_field = (local0 + downward).astype(jnp.bfloat16)
    far_field = jnp.einsum('lkm,lrk->rlm', basis_wide, leaf_field.astype(jnp.float32)).reshape(RHS, POINTS)
    return far_field + near_field(densities, points, weights, near_offsets)
```

```python
import functools
import math

import jax
import jax.numpy as jnp
from jax import lax
from jax.experimental import pallas as pl
from jax.experimental.pallas import tpu as pltpu
from jax.sharding import PartitionSpec as P

AXES = ("gx", "gy")
REACH = 8
WINDOW = 8
ROW = 8
core_square = 0.0004
four_pi = 4.0 * math.pi
f32 = jnp.float32
bf16 = jnp.bfloat16
VMEM_LIMIT = 40 << 20

SMEM = pl.BlockSpec(memory_space=pltpu.SMEM)
VMEM = pl.BlockSpec(memory_space=pltpu.VMEM)


def nt(a, b):
    return lax.dot_general(a, b, (((1,), (1,)), ((), ())), preferred_element_type=f32)


def low_half(shape):
    return lax.broadcasted_iota(jnp.int32, shape, len(shape) - 1) < 64


def pieces(x):
    first = x.astype(bf16)
    rest = x - first.astype(f32)
    second = rest.astype(bf16)
    third = (rest - second.astype(f32)).astype(bf16)
    return first, second, third


def upward_kernel(
    column_ref, lists_ref, dens_ref, points_ref, weights_ref, basis_ref, transfer_ref,
    pack_ref, below_ref, above_ref, own_ref, up_ref, down_ref, coarse_ref, both_ref,
):
    leaves = basis_ref.shape[0]
    rim = REACH * 128
    for part in range(4):
        span = pl.ds(part * 1024, 1024)
        scaled = dens_ref[:, span].astype(f32) * (weights_ref[:, span] * (1.0 / four_pi))
        pack_ref[0:16, span] = scaled.astype(bf16)
        one, two, three = pieces(points_ref[:, span])
        rows = jnp.concatenate(
            [one.astype(f32), two.astype(f32), three.astype(f32), jnp.zeros((7, 1024), f32)], axis=0
        )
        pack_ref[16:32, span] = rows.astype(bf16)
    below_ref[...] = pack_ref[:, -rim:]
    above_ref[...] = pack_ref[:, :rim]

    coarse = []
    for group in range(leaves // 8):
        total = jnp.zeros((16, 64), f32)
        for child in range(8):
            leaf = group * 8 + child
            basis = basis_ref[leaf]
            twice = nt(dens_ref[:, leaf * 128 : (leaf + 1) * 128], jnp.concatenate([basis, basis], axis=0))
            rounded = twice.astype(bf16)
            both_ref[leaf] = rounded
            total += jnp.dot(rounded[:, :64], transfer_ref[leaf], preferred_element_type=f32)
        coarse.append(total)
    for pair in range(len(coarse) // 2):
        tile = jnp.concatenate([coarse[2 * pair], coarse[2 * pair + 1]], axis=1).astype(bf16)
        coarse_ref[:, pair] = jnp.broadcast_to(tile[None], (coarse_ref.shape[0], 16, 128))

    column = column_ref[0]
    mask = low_half((16, 128))

    def fill(target, carry):
        for ref, window in (
            (own_ref, target - column + WINDOW),
            (up_ref, jnp.minimum(target - column + 2 * WINDOW, 2 * WINDOW)),
            (down_ref, jnp.maximum(target - column, 0)),
        ):
            for slot in range(8):
                ref[target, slot] = jnp.where(
                    mask, both_ref[lists_ref[slot, window]], both_ref[lists_ref[slot + 8, window]]
                )
        return carry

    lax.fori_loop(0, ROW, fill, 0)


def upward(column, lists, densities, points, weights, basis, transfer):
    count = densities.shape[1]
    leaves = basis.shape[0]
    block = jax.ShapeDtypeStruct((ROW, 8, 16, 128), bf16)
    return pl.pallas_call(
        upward_kernel,
        name="upward",
        out_shape=(
            jax.ShapeDtypeStruct((32, count), bf16),
            jax.ShapeDtypeStruct((32, REACH * 128), bf16),
            jax.ShapeDtypeStruct((32, REACH * 128), bf16),
            block, block, block,
            jax.ShapeDtypeStruct((128, leaves // 16, 16, 128), bf16),
        ),
        in_specs=[SMEM, SMEM, VMEM, VMEM, VMEM, VMEM, VMEM],
        out_specs=[VMEM] * 7,
        scratch_shapes=[pltpu.VMEM((leaves, 16, 128), bf16)],
        compiler_params=pltpu.CompilerParams(vmem_limit_bytes=VMEM_LIMIT),
        cost_estimate=pl.CostEstimate(flops=20_000_000, bytes_accessed=4 << 20, transcendentals=0),
    )(column, lists, densities, points, weights, basis, transfer)


def near_kernel(first, leaves, offsets_ref, pack_ref, below_ref, above_ref, near_ref, left_ref, right_ref, wide_ref):
    rim = REACH * 128
    inner = pack_ref.shape[1]

    def build(source, at, start, width, own):
        wide_ref[:, pl.ds(at, width)] = source[0:16, pl.ds(start, width)]
        rows = source[16:32, pl.ds(start, width)].astype(f32)
        one, two, three = rows[0:3], rows[3:6], rows[6:9]
        whole = (one + two) + three
        square = whole[0:1] * whole[0:1] + whole[1:2] * whole[1:2] + whole[2:3] * whole[2:3]
        ones = jnp.ones((3, width), f32)
        m1, m2, m3 = (p.astype(f32) for p in pieces(square))
        fill = jnp.zeros((8, width), f32)
        right = jnp.concatenate(
            [one, two, one, two, three, one, ones, m1, m2, m3, fill], axis=0
        )
        right_ref[:, pl.ds(at, width)] = right.astype(bf16)
        if own:
            n1, n2, n3 = (p.astype(f32) for p in pieces(square + core_square))
            left = jnp.concatenate(
                [-2 * one, -2 * one, -2 * two, -2 * two, -2 * one, -2 * three, n1, n2, n3, ones, fill], axis=0
            )
            left_ref[:, pl.ds(start, width)] = left.astype(bf16)

    for part in range(rim // 512):
        build(below_ref, part * 512, part * 512, 512, False)
        build(above_ref, rim + inner + part * 512, part * 512, 512, False)
    for part in range(inner // 512):
        build(pack_ref, rim + part * 512, part * 512, 512, True)

    slots = offsets_ref.shape[0]

    def one_leaf(step, carry):
        leaf = first + step
        own = left_ref[:, pl.ds(pl.multiple_of(leaf * 128, 128), 128)]
        total = jnp.zeros((16, 128), f32)
        for slot in range(0, slots, 2):
            spans = [
                pl.ds(pl.multiple_of((leaf + REACH + offsets_ref[s, leaf]) * 128, 128), 128)
                for s in range(slot, min(slot + 2, slots))
            ]
            right = jnp.concatenate([right_ref[:, span] for span in spans], axis=1)
            wide = jnp.concatenate([wide_ref[:, span] for span in spans], axis=1)
            square = lax.dot_general(own, right, (((0,), (0,)), ((), ())), preferred_element_type=f32)
            total += nt(wide, lax.rsqrt(square).astype(bf16))
        near_ref[:, pl.ds(pl.multiple_of(step * 128, 128), 128)] = total
        return carry

    lax.fori_loop(0, leaves, one_leaf, 0)


def near_field(offsets, pack, below, above, first, leaves):
    count = pack.shape[1]
    wide = count + 2 * REACH * 128
    points = leaves * 128 * offsets.shape[0] * 128
    return pl.pallas_call(
        functools.partial(near_kernel, first, leaves),
        name="near",
        out_shape=jax.ShapeDtypeStruct((16, leaves * 128), f32),
        in_specs=[SMEM, VMEM, VMEM, VMEM],
        out_specs=VMEM,
        scratch_shapes=[
            pltpu.VMEM((32, count), bf16),
            pltpu.VMEM((32, wide), bf16),
            pltpu.VMEM((16, wide), bf16),
        ],
        compiler_params=pltpu.CompilerParams(vmem_limit_bytes=VMEM_LIMIT),
        cost_estimate=pl.CostEstimate(flops=points * 96, bytes_accessed=1 << 20, transcendentals=points),
    )(offsets, pack, below, above)


def spread_matrix():
    row = lax.broadcasted_iota(jnp.int32, (128, 256), 0)
    col = lax.broadcasted_iota(jnp.int32, (128, 256), 1)
    hit = ((row // 64) == (col // 128)) & ((row % 64) == (col % 64))
    return jnp.where(hit, 1.0, 0.0).astype(bf16)


def coupled(coupling_ref, block, slots, pick):
    mask = low_half((16, 128))
    rows = [jnp.where(mask, pick(s), pick(s + 1)) for s in range(0, slots, 2)]
    left = jnp.concatenate(rows, axis=1)
    right = jnp.concatenate([coupling_ref[block, s] for s in range(slots)], axis=1)
    return nt(left, right)


def leaf_kernel(column_ref, refs_ref, swapped_ref, below_ref, above_ref, coupling_ref, local_ref, table_ref):
    step = pl.program_id(0)
    per_step, slots = coupling_ref.shape[:2]

    @pl.when(step == 0)
    def _():
        column = column_ref[0]
        spread = spread_matrix()

        def put(window, tiles):
            out = jnp.dot(tiles.reshape(8 * 16, 128), spread, preferred_element_type=f32).astype(bf16)
            out = out.reshape(8, 16, 256)
            table_ref[pl.ds(window * 16, 8)] = out[:, :, :128]
            table_ref[pl.ds(window * 16 + 8, 8)] = out[:, :, 128:]

        put(0, below_ref[column])
        put(2 * WINDOW, above_ref[column])
        for window in range(1, 2 * WINDOW):
            place = column + window
            owner = lax.rem(place, ROW)
            crossed = jnp.where((place >= ROW) & (place < 2 * ROW), 0, 1)
            put(window, swapped_ref[owner, crossed])

    for block in range(per_step):
        leaf = step * per_step + block
        local_ref[block] = coupled(
            coupling_ref, block, slots, lambda s: table_ref[refs_ref[leaf, s]]
        )


def leaf_local(column, refs, swapped, below, above, coupling):
    leaves, slots = coupling.shape[:2]
    per_step = 4
    table = (2 * WINDOW + 1) * 16
    return pl.pallas_call(
        leaf_kernel,
        name="leaf_local",
        out_shape=jax.ShapeDtypeStruct((leaves, 16, 64), f32),
        grid_spec=pltpu.PrefetchScalarGridSpec(
            num_scalar_prefetch=2,
            grid=(leaves // per_step,),
            in_specs=[
                VMEM, VMEM, VMEM,
                pl.BlockSpec((per_step, slots, 64, 64), lambda i, *_: (i, 0, 0, 0)),
            ],
            out_specs=pl.BlockSpec((per_step, 16, 64), lambda i, *_: (i, 0, 0)),
            scratch_shapes=[pltpu.VMEM((table, 16, 128), bf16)],
        ),
        compiler_params=pltpu.CompilerParams(vmem_limit_bytes=VMEM_LIMIT),
        cost_estimate=pl.CostEstimate(flops=leaves * slots * 64 * 64 * 32, bytes_accessed=18 << 20, transcendentals=0),
    )(column, refs, swapped, below, above, coupling)


def downward_kernel(
    refs_ref, coarse_ref, coupling_ref, transfer_ref, basis_ref, local_ref, near_ref, out_ref, picked_ref
):
    groups, slots = coupling_ref.shape[:2]
    mask = low_half((16, 128))
    for group in range(groups):
        for slot in range(slots):
            ref = refs_ref[group, slot]
            tile = coarse_ref[ref // 4, lax.rem(ref, 4) // 2]
            keep = mask == (lax.rem(ref, 2) == 0)
            picked_ref[group * slots + slot] = jnp.where(keep, tile, jnp.zeros_like(tile))
    row = lax.broadcasted_iota(jnp.int32, (128, 128), 0)
    col = lax.broadcasted_iota(jnp.int32, (128, 128), 1)
    fold = jnp.where((row % 64) == (col % 64), 1.0, 0.0).astype(bf16)
    for group in range(groups):
        tiles = picked_ref[pl.ds(group * slots, slots)].reshape(slots * 16, 128)
        both = jnp.dot(tiles, fold, preferred_element_type=f32).astype(bf16).reshape(slots, 16, 128)
        local1 = coupled(coupling_ref, group, slots, lambda s: both[s]).astype(bf16)
        for child in range(8):
            leaf = group * 8 + child
            field = (local_ref[leaf] + nt(local1, transfer_ref[leaf])).astype(bf16)
            span = slice(leaf * 128, (leaf + 1) * 128)
            out_ref[:, span] = near_ref[:, span] + jnp.dot(
                field, basis_ref[leaf], preferred_element_type=f32
            )


def downward(refs, coarse, coupling, transfer, basis, local0, near):
    groups, slots = coupling.shape[:2]
    return pl.pallas_call(
        downward_kernel,
        name="downward",
        out_shape=jax.ShapeDtypeStruct(near.shape, f32),
        in_specs=[SMEM] + [VMEM] * 6,
        out_specs=VMEM,
        scratch_shapes=[pltpu.VMEM((groups * slots, 16, 128), bf16)],
        compiler_params=pltpu.CompilerParams(vmem_limit_bytes=VMEM_LIMIT),
        cost_estimate=pl.CostEstimate(flops=60_000_000, bytes_accessed=4 << 20, transcendentals=0),
    )(refs, coarse, coupling, transfer, basis, local0, near)


def shifted(shard, by, devices):
    return lax.ppermute(shard, AXES, [(i, i + by) for i in range(devices) if 0 <= i + by < devices])


def local(
    densities, points, weights, near_offsets, leaf_basis, transfer, send_lists, relay_refs, leaf_coupling,
    coarse_refs, coarse_coupling,
):
    devices = lax.axis_size(AXES)
    column = lax.rem(lax.axis_index("gy").astype(jnp.int32), ROW).reshape(1)
    rows = [[row * ROW + i for i in range(ROW)] for row in range(devices // ROW)]
    pack, rim_last, rim_first, own, up, down, coarse = upward(
        column, send_lists[0].T, densities, points, weights[None, :], leaf_basis, transfer
    )
    everyone = lax.all_to_all(coarse, AXES, 0, 0, tiled=True)
    from_below = shifted(rim_last, 1, devices)
    from_above = shifted(rim_first, -1, devices)
    lists_below = shifted(up, ROW, devices)
    lists_above = shifted(down, -ROW, devices)
    crossing = jnp.where(
        jnp.arange(ROW, dtype=jnp.int32)[:, None, None, None] < column[0], lists_below, lists_above
    )
    swapped = lax.all_to_all(
        jnp.stack([own, crossing], axis=1), AXES, 0, 0, axis_index_groups=rows, tiled=True
    )
    near = near_field(near_offsets.T, pack, from_below, from_above, 0, near_offsets.shape[0])
    local0 = leaf_local(column, relay_refs, swapped, lists_below, lists_above, leaf_coupling)
    return downward(coarse_refs, everyone, coarse_coupling, transfer, leaf_basis, local0, near)


def solution(mesh):
    in_specs = (
        P(None, AXES),
        P(None, AXES),
        P(AXES),
        P(AXES, None),
        P(AXES, None, None),
        P(AXES, None, None),
        P(AXES, None, None),
        P(AXES, None),
        P(AXES, None, None, None),
        P(AXES, None),
        P(AXES, None, None, None),
    )
    return jax.shard_map(local, mesh=mesh, in_specs=in_specs, out_specs=P(None, AXES), check_vma=False)
```

```python
import functools
import math

import jax
import jax.numpy as jnp
from jax import lax
from jax.experimental import pallas as pl
from jax.experimental.pallas import tpu as pltpu
from jax.sharding import PartitionSpec as P

AXES = ("gx", "gy")
REACH = 8
WINDOW = 8
ROW = 8
core_square = 0.0004
four_pi = 4.0 * math.pi
f32 = jnp.float32
bf16 = jnp.bfloat16

SMEM = pl.BlockSpec(memory_space=pltpu.SMEM)
HBM = pl.BlockSpec(memory_space=pltpu.HBM)
VMEM = pl.BlockSpec(memory_space=pltpu.VMEM)


def nt(a, b):
    return lax.dot_general(a, b, (((1,), (1,)), ((), ())), preferred_element_type=f32)


def low_half(shape):
    return lax.broadcasted_iota(jnp.int32, shape, len(shape) - 1) < 64


def pieces(x):
    first = x.astype(bf16)
    rest = x - first.astype(f32)
    second = rest.astype(bf16)
    third = (rest - second.astype(f32)).astype(bf16)
    return first, second, third


def upward_kernel(
    column_ref, lists_ref, dens_hbm, points_hbm, weights_hbm, basis_hbm, transfer_hbm,
    pack_ref, below_ref, above_ref, own_ref, up_ref, down_ref, coarse_ref,
    dens_ref, points_ref, weights_ref, basis_ref, transfer_ref, both_ref, sems,
):
    copies = [
        pltpu.make_async_copy(source, target, sems.at[i])
        for i, (source, target) in enumerate((
            (dens_hbm, dens_ref), (points_hbm, points_ref), (weights_hbm, weights_ref),
            (basis_hbm, basis_ref), (transfer_hbm, transfer_ref),
        ))
    ]
    for copy in copies:
        copy.start()
    for copy in copies[:3]:
        copy.wait()
    leaves = basis_ref.shape[0]
    rim = REACH * 128
    for part in range(4):
        span = pl.ds(part * 1024, 1024)
        scaled = dens_ref[:, span].astype(f32) * (weights_ref[:, span] * (1.0 / four_pi))
        pack_ref[0:16, span] = scaled.astype(bf16)
        one, two, three = pieces(points_ref[:, span])
        rows = jnp.concatenate(
            [one.astype(f32), two.astype(f32), three.astype(f32), jnp.zeros((7, 1024), f32)], axis=0
        )
        pack_ref[16:32, span] = rows.astype(bf16)
    below_ref[...] = pack_ref[:, -rim:]
    above_ref[...] = pack_ref[:, :rim]

    for copy in copies[3:]:
        copy.wait()
    coarse = []
    for group in range(leaves // 8):
        total = jnp.zeros((16, 64), f32)
        for child in range(8):
            leaf = group * 8 + child
            basis = basis_ref[leaf]
            twice = nt(dens_ref[:, leaf * 128 : (leaf + 1) * 128], jnp.concatenate([basis, basis], axis=0))
            rounded = twice.astype(bf16)
            both_ref[leaf] = rounded
            total += jnp.dot(rounded[:, :64], transfer_ref[leaf], preferred_element_type=f32)
        coarse.append(total)
    for pair in range(len(coarse) // 2):
        tile = jnp.concatenate([coarse[2 * pair], coarse[2 * pair + 1]], axis=1).astype(bf16)
        coarse_ref[:, pair] = jnp.broadcast_to(tile[None], (coarse_ref.shape[0], 16, 128))

    column = column_ref[0]
    mask = low_half((16, 128))

    def fill(target, carry):
        for ref, window in (
            (own_ref, target - column + WINDOW),
            (up_ref, jnp.minimum(target - column + 2 * WINDOW, 2 * WINDOW)),
            (down_ref, jnp.maximum(target - column, 0)),
        ):
            for slot in range(8):
                ref[target, slot] = jnp.where(
                    mask, both_ref[lists_ref[slot, window]], both_ref[lists_ref[slot + 8, window]]
                )
        return carry

    lax.fori_loop(0, ROW, fill, 0)


def upward(column, lists, densities, points, weights, basis, transfer, row_count):
    count = densities.shape[1]
    leaves = basis.shape[0]
    block = jax.ShapeDtypeStruct((ROW, 8, 16, 128), bf16)
    return pl.pallas_call(
        upward_kernel,
        name="upward",
        out_shape=(
            jax.ShapeDtypeStruct((32, count), bf16),
            jax.ShapeDtypeStruct((32, REACH * 128), bf16),
            jax.ShapeDtypeStruct((32, REACH * 128), bf16),
            block, block, block,
            jax.ShapeDtypeStruct((row_count, leaves // 16, 16, 128), bf16),
        ),
        in_specs=[SMEM, SMEM] + [HBM] * 5,
        out_specs=[VMEM] * 7,
        scratch_shapes=[
            pltpu.VMEM(densities.shape, bf16),
            pltpu.VMEM(points.shape, f32),
            pltpu.VMEM(weights.shape, f32),
            pltpu.VMEM(basis.shape, bf16),
            pltpu.VMEM(transfer.shape, bf16),
            pltpu.VMEM((leaves, 16, 128), bf16),
            pltpu.SemaphoreType.DMA((5,)),
        ],
        compiler_params=pltpu.CompilerParams(vmem_limit_bytes=12 << 20),
        cost_estimate=pl.CostEstimate(flops=20_000_000, bytes_accessed=4 << 20, transcendentals=0),
    )(column, lists, *(pltpu.with_memory_space_constraint(x, pltpu.HBM) for x in (densities, points, weights, basis, transfer)))


def near_kernel(
    offsets_ref, pack_ref, below_ref, above_ref, coupling_hbm,
    near_hbm, packed_hbm, near_ref, left_ref, right_ref, wide_ref, buffer_ref, packed_ref, sems, out_sems,
):
    rim = REACH * 128
    inner = pack_ref.shape[1]
    leaves, tiles = coupling_hbm.shape[:2]
    per_step = buffer_ref.shape[1]
    steps = leaves // per_step

    def fetch(step, slot):
        return pltpu.make_async_copy(
            coupling_hbm.at[pl.ds(step * per_step, per_step)], buffer_ref.at[slot], sems.at[slot]
        )

    def flush(step, slot):
        return pltpu.make_async_copy(
            packed_ref.at[slot], packed_hbm.at[pl.ds(step * per_step, per_step)], out_sems.at[slot]
        )

    fetch(0, 0).start()

    def build(source, at, start, width, own):
        wide_ref[:, pl.ds(at, width)] = source[0:16, pl.ds(start, width)]
        rows = source[16:32, pl.ds(start, width)].astype(f32)
        one, two, three = rows[0:3], rows[3:6], rows[6:9]
        whole = (one + two) + three
        square = whole[0:1] * whole[0:1] + whole[1:2] * whole[1:2] + whole[2:3] * whole[2:3]
        ones = jnp.ones((3, width), f32)
        m1, m2, m3 = (p.astype(f32) for p in pieces(square))
        fill = jnp.zeros((8, width), f32)
        right = jnp.concatenate([one, two, one, two, three, one, ones, m1, m2, m3, fill], axis=0)
        right_ref[:, pl.ds(at, width)] = right.astype(bf16)
        if own:
            n1, n2, n3 = (p.astype(f32) for p in pieces(square + core_square))
            left = jnp.concatenate(
                [-2 * one, -2 * one, -2 * two, -2 * two, -2 * one, -2 * three, n1, n2, n3, ones, fill], axis=0
            )
            left_ref[:, pl.ds(start, width)] = left.astype(bf16)

    for part in range(rim // 512):
        build(below_ref, part * 512, part * 512, 512, False)
        build(above_ref, rim + inner + part * 512, part * 512, 512, False)
    for part in range(inner // 512):
        build(pack_ref, rim + part * 512, part * 512, 512, True)

    slots = offsets_ref.shape[0]

    def one_leaf(leaf):
        own = left_ref[:, pl.ds(pl.multiple_of(leaf * 128, 128), 128)]
        total = jnp.zeros((16, 128), f32)
        for slot in range(0, slots, 2):
            spans = [
                pl.ds(pl.multiple_of((leaf + REACH + offsets_ref[s, leaf]) * 128, 128), 128)
                for s in range(slot, min(slot + 2, slots))
            ]
            right = jnp.concatenate([right_ref[:, span] for span in spans], axis=1)
            wide = jnp.concatenate([wide_ref[:, span] for span in spans], axis=1)
            square = lax.dot_general(own, right, (((0,), (0,)), ((), ())), preferred_element_type=f32)
            total += nt(wide, lax.rsqrt(square).astype(bf16))
        near_ref[:, pl.ds(pl.multiple_of(leaf * 128, 128), 128)] = total

    def one_step(step, carry):
        slot = lax.rem(step, 2)
        fetch(step, slot).wait()

        @pl.when(step + 1 < steps)
        def _():
            fetch(step + 1, 1 - slot).start()

        @pl.when(step >= 2)
        def _():
            flush(step - 2, slot).wait()

        for inside in range(per_step):
            leaf = step * per_step + inside
            one_leaf(leaf)
            for tile in range(0, tiles, 2):
                packed_ref[slot, inside, :, tile * 64 : (tile + 2) * 64] = jnp.concatenate(
                    [buffer_ref[slot, inside, tile], buffer_ref[slot, inside, tile + 1]], axis=1
                )
        flush(step, slot).start()
        return carry

    lax.fori_loop(0, steps, one_step, 0)
    last = pltpu.make_async_copy(near_ref, near_hbm, out_sems.at[2])
    last.start()
    for step in range(steps - 2, steps):
        flush(step, step % 2).wait()
    last.wait()


def near_field(offsets, pack, below, above, coupling):
    count = pack.shape[1]
    wide = count + 2 * REACH * 128
    leaves, tiles = coupling.shape[:2]
    per_step = 4
    points = count * offsets.shape[0] * 128
    return pl.pallas_call(
        near_kernel,
        name="near",
        out_shape=(
            pltpu.HBM((16, count), f32),
            pltpu.HBM((leaves, 64, tiles * 64), bf16),
        ),
        in_specs=[SMEM, VMEM, VMEM, VMEM, HBM],
        out_specs=[HBM, HBM],
        scratch_shapes=[
            pltpu.VMEM((16, count), f32),
            pltpu.VMEM((32, count), bf16),
            pltpu.VMEM((32, wide), bf16),
            pltpu.VMEM((16, wide), bf16),
            pltpu.VMEM((2, per_step) + coupling.shape[1:], bf16),
            pltpu.VMEM((2, per_step, 64, tiles * 64), bf16),
            pltpu.SemaphoreType.DMA((2,)),
            pltpu.SemaphoreType.DMA((3,)),
        ],
        compiler_params=pltpu.CompilerParams(vmem_limit_bytes=24 << 20),
        cost_estimate=pl.CostEstimate(flops=points * 96, bytes_accessed=28 << 20, transcendentals=points),
    )(offsets, pack, below, above, pltpu.with_memory_space_constraint(coupling, pltpu.HBM))


def assemble_kernel(column_ref, own_ref, below_ref, above_ref, coarse_ref, out_ref):
    column = column_ref[0]
    rows, pairs = coarse_ref.shape[:2]
    for target in range(out_ref.shape[0]):
        out_ref[target, 0:8] = own_ref[target]
        crossed = jnp.where(target < column, 0, 1)

        @pl.when(crossed == 0)
        def _():
            out_ref[target, 8:16] = below_ref[target]

        @pl.when(crossed == 1)
        def _():
            out_ref[target, 8:16] = above_ref[target]

        out_ref[target, 16:] = coarse_ref[...].reshape(rows * pairs, 16, 128)


def assemble(column, own, below, above, coarse):
    rows, pairs = coarse.shape[:2]
    return pl.pallas_call(
        assemble_kernel,
        name="assemble",
        out_shape=jax.ShapeDtypeStruct((ROW, 16 + rows * pairs, 16, 128), bf16),
        in_specs=[SMEM] + [VMEM] * 4,
        out_specs=VMEM,
        compiler_params=pltpu.CompilerParams(vmem_limit_bytes=8 << 20),
        cost_estimate=pl.CostEstimate(flops=0, bytes_accessed=3 << 20, transcendentals=0),
    )(column, own, below, above, coarse)


def spread_matrix():
    row = lax.broadcasted_iota(jnp.int32, (128, 256), 0)
    col = lax.broadcasted_iota(jnp.int32, (128, 256), 1)
    hit = ((row // 64) == (col // 128)) & ((row % 64) == (col % 64))
    return jnp.where(hit, 1.0, 0.0).astype(bf16)


def paired(slots, pick):
    mask = low_half((16, 128))
    return jnp.concatenate([jnp.where(mask, pick(s), pick(s + 1)) for s in range(0, slots, 2)], axis=1)


def finish_kernel(
    column_ref, leaf_refs, group_refs, swapped_ref, below_ref, above_ref,
    coupling_hbm, transfer_hbm, basis_hbm, near_hbm, packed_hbm,
    out_ref, coupling_ref, transfer_ref, basis_ref, near_ref, packed_ref, table_ref, picked_ref, local1_ref, sems,
):
    copies = [
        pltpu.make_async_copy(source, target, sems.at[i])
        for i, (source, target) in enumerate((
            (coupling_hbm, coupling_ref), (transfer_hbm, transfer_ref), (basis_hbm, basis_ref),
            (near_hbm, near_ref), (packed_hbm, packed_ref),
        ))
    ]
    for copy in copies:
        copy.start()
    groups, slots = coupling_ref.shape[:2]
    mask = low_half((16, 128))
    column = column_ref[0]
    spread = spread_matrix()

    def put(window, tiles):
        out = jnp.dot(tiles.reshape(8 * 16, 128), spread, preferred_element_type=f32).astype(bf16)
        out = out.reshape(8, 16, 256)
        table_ref[pl.ds(window * 16, 8)] = out[:, :, :128]
        table_ref[pl.ds(window * 16 + 8, 8)] = out[:, :, 128:]

    put(0, below_ref[column])
    put(2 * WINDOW, above_ref[column])
    for window in range(1, 2 * WINDOW):
        place = column + window
        owner = place & (ROW - 1)
        crossed = jnp.where((place >= ROW) & (place < 2 * ROW), 0, 8)
        put(window, swapped_ref[owner, pl.ds(pl.multiple_of(crossed, 8), 8)])

    for group in range(groups):
        for slot in range(slots):
            ref = group_refs[group, slot]
            tile = swapped_ref[(ref >> 2) & (ROW - 1), 16 + ((ref >> 5) << 1) + ((ref >> 1) & 1)]
            keep = mask == ((ref & 1) == 0)
            picked_ref[group * slots + slot] = jnp.where(keep, tile, jnp.zeros_like(tile))
    row = lax.broadcasted_iota(jnp.int32, (128, 128), 0)
    col = lax.broadcasted_iota(jnp.int32, (128, 128), 1)
    fold = jnp.where((row % 64) == (col % 64), 1.0, 0.0).astype(bf16)
    copies[0].wait()
    for group in range(groups):
        tiles = picked_ref[pl.ds(group * slots, slots)].reshape(slots * 16, 128)
        both = jnp.dot(tiles, fold, preferred_element_type=f32).astype(bf16).reshape(slots, 16, 128)
        wide = jnp.concatenate([coupling_ref[group, s] for s in range(slots)], axis=1)
        local1_ref[group] = nt(paired(slots, lambda s: both[s]), wide).astype(bf16)

    for copy in copies[1:]:
        copy.wait()

    def one_group(group, carry):
        for child in range(8):
            leaf = group * 8 + child
            field = nt(paired(slots, lambda s: table_ref[leaf_refs[leaf, s]]), packed_ref[leaf])
            field = (field + nt(local1_ref[group], transfer_ref[leaf])).astype(bf16)
            span = pl.ds(pl.multiple_of(leaf * 128, 128), 128)
            out_ref[:, span] = near_ref[:, span] + jnp.dot(field, basis_ref[leaf], preferred_element_type=f32)
        return carry

    lax.fori_loop(0, groups, one_group, 0)


def finish(column, leaf_refs, group_refs, swapped, below, above, packed, coupling, transfer, basis, near):
    groups, slots = coupling.shape[:2]
    return pl.pallas_call(
        finish_kernel,
        name="finish",
        out_shape=jax.ShapeDtypeStruct(near.shape, f32),
        in_specs=[SMEM] * 3 + [VMEM] * 3 + [HBM] * 5,
        out_specs=VMEM,
        scratch_shapes=[
            pltpu.VMEM(coupling.shape, bf16),
            pltpu.VMEM(transfer.shape, bf16),
            pltpu.VMEM(basis.shape, bf16),
            pltpu.VMEM(near.shape, f32),
            pltpu.VMEM(packed.shape, bf16),
            pltpu.VMEM(((2 * WINDOW + 1) * 16, 16, 128), bf16),
            pltpu.VMEM((groups * slots, 16, 128), bf16),
            pltpu.VMEM((groups, 16, 64), bf16),
            pltpu.SemaphoreType.DMA((5,)),
        ],
        compiler_params=pltpu.CompilerParams(vmem_limit_bytes=24 << 20),
        cost_estimate=pl.CostEstimate(flops=200_000_000, bytes_accessed=14 << 20, transcendentals=0),
    )(
        column, leaf_refs, group_refs, swapped, below, above,
        *(pltpu.with_memory_space_constraint(x, pltpu.HBM) for x in (coupling, transfer, basis, near, packed)),
    )


def shifted(shard, by, devices):
    return lax.ppermute(shard, AXES, [(i, i + by) for i in range(devices) if 0 <= i + by < devices])


def local(
    densities, points, weights, near_offsets, leaf_basis, transfer, send_lists, relay_refs, leaf_coupling,
    coarse_refs, coarse_coupling,
):
    devices = lax.axis_size(AXES)
    column = lax.rem(lax.axis_index("gy").astype(jnp.int32), ROW).reshape(1)
    rows = [[row * ROW + i for i in range(ROW)] for row in range(devices // ROW)]
    columns = [[col + ROW * i for i in range(devices // ROW)] for col in range(ROW)]
    pack, rim_last, rim_first, own, up, down, coarse = upward(
        column, send_lists[0].T, densities, points, weights[None, :], leaf_basis, transfer, devices // ROW
    )
    coarse_rows = lax.all_to_all(coarse, AXES, 0, 0, axis_index_groups=columns, tiled=True)
    lists_below = shifted(up, ROW, devices)
    lists_above = shifted(down, -ROW, devices)
    from_below = shifted(rim_last, 1, devices)
    from_above = shifted(rim_first, -1, devices)
    payload = assemble(column, own, lists_below, lists_above, coarse_rows)
    payload, from_below, from_above = lax.optimization_barrier((payload, from_below, from_above))
    swapped = lax.all_to_all(payload, AXES, 0, 0, axis_index_groups=rows, tiled=True)
    near, packed = near_field(near_offsets.T, pack, from_below, from_above, leaf_coupling)
    return finish(
        column, relay_refs, coarse_refs, swapped, lists_below, lists_above, packed, coarse_coupling, transfer,
        leaf_basis, near,
    )


def solution(mesh):
    in_specs = (
        P(None, AXES),
        P(None, AXES),
        P(AXES),
        P(AXES, None),
        P(AXES, None, None),
        P(AXES, None, None),
        P(AXES, None, None),
        P(AXES, None),
        P(AXES, None, None, None),
        P(AXES, None),
        P(AXES, None, None, None),
    )
    return jax.shard_map(local, mesh=mesh, in_specs=in_specs, out_specs=P(None, AXES), check_vma=False)
```

```python
import functools
import math

import jax
import jax.numpy as jnp
from jax import lax
from jax.experimental import pallas as pl
from jax.experimental.pallas import tpu as pltpu
from jax.sharding import PartitionSpec as P

AXES = ("gx", "gy")
REACH = 8
WINDOW = 8
DEPTH = 2
ROW = 8
core_square = 0.0004
four_pi = 4.0 * math.pi
f32 = jnp.float32
bf16 = jnp.bfloat16

SMEM = pl.BlockSpec(memory_space=pltpu.SMEM)
HBM = pl.BlockSpec(memory_space=pltpu.HBM)
VMEM = pl.BlockSpec(memory_space=pltpu.VMEM)


def nt(a, b):
    return lax.dot_general(a, b, (((1,), (1,)), ((), ())), preferred_element_type=f32)


def low_half(shape):
    return lax.broadcasted_iota(jnp.int32, shape, len(shape) - 1) < 64


def pieces(x):
    first = x.astype(bf16)
    rest = x - first.astype(f32)
    second = rest.astype(bf16)
    third = (rest - second.astype(f32)).astype(bf16)
    return first, second, third


def upward_kernel(
    column_ref, lists_ref, dens_hbm, points_hbm, weights_hbm, basis_hbm, transfer_hbm,
    pack_ref, below_ref, above_ref, own_ref, up_ref, down_ref, coarse_ref,
    dens_ref, points_ref, weights_ref, basis_ref, transfer_ref, both_ref, sems,
):
    copies = [
        pltpu.make_async_copy(source, target, sems.at[i])
        for i, (source, target) in enumerate((
            (dens_hbm, dens_ref), (points_hbm, points_ref), (weights_hbm, weights_ref),
            (basis_hbm, basis_ref), (transfer_hbm, transfer_ref),
        ))
    ]
    for copy in copies:
        copy.start()
    for copy in copies[:3]:
        copy.wait()
    leaves = basis_ref.shape[0]
    rim = REACH * 128
    for part in range(4):
        span = pl.ds(part * 1024, 1024)
        scaled = dens_ref[:, span].astype(f32) * (weights_ref[:, span] * (1.0 / four_pi))
        pack_ref[0:16, span] = scaled.astype(bf16)
        one, two, three = pieces(points_ref[:, span])
        rows = jnp.concatenate(
            [one.astype(f32), two.astype(f32), three.astype(f32), jnp.zeros((7, 1024), f32)], axis=0
        )
        pack_ref[16:32, span] = rows.astype(bf16)
    below_ref[...] = pack_ref[:, -rim:]
    above_ref[...] = pack_ref[:, :rim]

    for copy in copies[3:]:
        copy.wait()
    coarse = []
    for group in range(leaves // 8):
        members = range(group * 8, group * 8 + 8)
        twice = [
            nt(dens_ref[:, leaf * 128 : (leaf + 1) * 128], jnp.concatenate([basis_ref[leaf]] * 2, axis=0)).astype(bf16)
            for leaf in members
        ]
        total = jnp.zeros((16, 64), f32)
        for leaf, rounded in zip(members, twice):
            both_ref[leaf] = rounded
            total += jnp.dot(rounded[:, :64], transfer_ref[leaf], preferred_element_type=f32)
        coarse.append(total)
    for pair in range(len(coarse) // 2):
        tile = jnp.concatenate([coarse[2 * pair], coarse[2 * pair + 1]], axis=1).astype(bf16)
        coarse_ref[:, pair] = jnp.broadcast_to(tile[None], (coarse_ref.shape[0], 16, 128))

    column = column_ref[0]
    mask = low_half((16, 128))

    def fill(target, carry):
        for ref, window in (
            (own_ref, target - column + WINDOW),
            (up_ref, jnp.minimum(target - column + 2 * WINDOW, 2 * WINDOW)),
            (down_ref, jnp.maximum(target - column, 0)),
        ):
            for slot in range(8):
                ref[target, slot] = jnp.where(
                    mask, both_ref[lists_ref[slot, window]], both_ref[lists_ref[slot + 8, window]]
                )
        return carry

    lax.fori_loop(0, ROW, fill, 0)


def upward(column, lists, densities, points, weights, basis, transfer, row_count):
    count = densities.shape[1]
    leaves = basis.shape[0]
    block = jax.ShapeDtypeStruct((ROW, 8, 16, 128), bf16)
    return pl.pallas_call(
        upward_kernel,
        name="upward",
        out_shape=(
            jax.ShapeDtypeStruct((32, count), bf16),
            jax.ShapeDtypeStruct((32, REACH * 128), bf16),
            jax.ShapeDtypeStruct((32, REACH * 128), bf16),
            block, block, block,
            jax.ShapeDtypeStruct((row_count, leaves // 16, 16, 128), bf16),
        ),
        in_specs=[SMEM, SMEM] + [HBM] * 5,
        out_specs=[VMEM] * 7,
        scratch_shapes=[
            pltpu.VMEM(densities.shape, bf16),
            pltpu.VMEM(points.shape, f32),
            pltpu.VMEM(weights.shape, f32),
            pltpu.VMEM(basis.shape, bf16),
            pltpu.VMEM(transfer.shape, bf16),
            pltpu.VMEM((leaves, 16, 128), bf16),
            pltpu.SemaphoreType.DMA((5,)),
        ],
        compiler_params=pltpu.CompilerParams(vmem_limit_bytes=12 << 20),
        cost_estimate=pl.CostEstimate(flops=20_000_000, bytes_accessed=4 << 20, transcendentals=0),
    )(column, lists, *(pltpu.with_memory_space_constraint(x, pltpu.HBM) for x in (densities, points, weights, basis, transfer)))


def near_kernel(
    first, leaves, offsets_ref, pack_ref, below_ref, above_ref, coupling_hbm,
    near_hbm, packed_hbm, near_ref, left_ref, right_ref, wide_ref, buffer_ref, packed_ref, sems, out_sems, last_sem,
):
    rim = REACH * 128
    inner = pack_ref.shape[1]
    tiles = coupling_hbm.shape[1]
    per_step = buffer_ref.shape[1]
    steps = leaves // per_step

    def fetch(step, slot):
        return [
            pltpu.make_async_copy(
                coupling_hbm.at[first + step * per_step + i], buffer_ref.at[slot, i], sems.at[slot, i]
            )
            for i in range(per_step)
        ]

    def flush(step, slot):
        return [
            pltpu.make_async_copy(
                packed_ref.at[slot, i], packed_hbm.at[step * per_step + i], out_sems.at[slot, i]
            )
            for i in range(per_step)
        ]

    for copy in fetch(0, 0):
        copy.start()

    def build(source, at, start, width, own):
        wide_ref[:, pl.ds(at, width)] = source[0:16, pl.ds(start, width)]
        rows = source[16:32, pl.ds(start, width)].astype(f32)
        one, two, three = rows[0:3], rows[3:6], rows[6:9]
        whole = (one + two) + three
        square = whole[0:1] * whole[0:1] + whole[1:2] * whole[1:2] + whole[2:3] * whole[2:3]
        ones = jnp.ones((3, width), f32)
        m1, m2, m3 = (p.astype(f32) for p in pieces(square))
        fill = jnp.zeros((8, width), f32)
        right = jnp.concatenate([one, two, one, two, three, one, ones, m1, m2, m3, fill], axis=0)
        right_ref[:, pl.ds(at, width)] = right.astype(bf16)
        if own:
            n1, n2, n3 = (p.astype(f32) for p in pieces(square + core_square))
            left = jnp.concatenate(
                [-2 * one, -2 * one, -2 * two, -2 * two, -2 * one, -2 * three, n1, n2, n3, ones, fill], axis=0
            )
            left_ref[:, pl.ds(start, width)] = left.astype(bf16)

    for part in range(rim // 512):
        build(below_ref, part * 512, part * 512, 512, False)
        build(above_ref, rim + inner + part * 512, part * 512, 512, False)
    for part in range(inner // 512):
        build(pack_ref, rim + part * 512, part * 512, 512, True)

    slots = offsets_ref.shape[0]

    def squares(leaf, slot):
        own = left_ref[:, pl.ds(pl.multiple_of(leaf * 128, 128), 128)]
        spans = [
            pl.ds(pl.multiple_of((leaf + REACH + offsets_ref[s, leaf]) * 128, 128), 128)
            for s in range(slot, min(slot + 2, slots))
        ]
        right = jnp.concatenate([right_ref[:, span] for span in spans], axis=1)
        wide = jnp.concatenate([wide_ref[:, span] for span in spans], axis=1)
        return wide, lax.dot_general(own, right, (((0,), (0,)), ((), ())), preferred_element_type=f32)

    def one_step(step, carry):
        slot = lax.rem(step, 2)
        for copy in fetch(step, slot):
            copy.wait()

        @pl.when(step + 1 < steps)
        def _():
            for copy in fetch(step + 1, 1 - slot):
                copy.start()

        @pl.when(step >= 2)
        def _():
            for copy in flush(step - 2, slot):
                copy.wait()

        work = [(inside, s) for inside in range(per_step) for s in range(0, slots, 2)]
        totals = [jnp.zeros((16, 128), f32)] * per_step
        ahead = [squares(first + step * per_step + inside, s) for inside, s in work[:DEPTH]]
        for at, (inside, s) in enumerate(work):
            leaf = step * per_step + inside
            if at + DEPTH < len(work):
                later, other = work[at + DEPTH]
                ahead.append(squares(first + step * per_step + later, other))
            wide, square = ahead.pop(0)
            totals[inside] += nt(wide, lax.rsqrt(square).astype(bf16))
            for tile in range(s * 2, min(s * 2 + 4, tiles), 2) if s < slots - 1 else range(s * 2, tiles, 2):
                packed_ref[slot, inside, :, tile * 64 : (tile + 2) * 64] = jnp.concatenate(
                    [buffer_ref[slot, inside, tile], buffer_ref[slot, inside, tile + 1]], axis=1
                )
            if s + 2 >= slots:
                near_ref[:, pl.ds(pl.multiple_of(leaf * 128, 128), 128)] = totals[inside]
        for copy in flush(step, slot):
            copy.start()
        return carry

    lax.fori_loop(0, steps, one_step, 0)
    last = pltpu.make_async_copy(near_ref, near_hbm, last_sem)
    last.start()
    for step in range(steps - 2, steps):
        for copy in flush(step, step % 2):
            copy.wait()
    last.wait()


def near_field(offsets, pack, below, above, coupling, first, leaves):
    count = pack.shape[1]
    wide = count + 2 * REACH * 128
    tiles = coupling.shape[1]
    per_step = 4
    points = leaves * 128 * offsets.shape[0] * 128
    return pl.pallas_call(
        functools.partial(near_kernel, first, leaves),
        name="near",
        out_shape=(
            pltpu.HBM((16, leaves * 128), f32),
            pltpu.HBM((leaves, 64, tiles * 64), bf16),
        ),
        in_specs=[SMEM, VMEM, VMEM, VMEM, HBM],
        out_specs=[HBM, HBM],
        scratch_shapes=[
            pltpu.VMEM((16, leaves * 128), f32),
            pltpu.VMEM((32, count), bf16),
            pltpu.VMEM((32, wide), bf16),
            pltpu.VMEM((16, wide), bf16),
            pltpu.VMEM((2, per_step) + coupling.shape[1:], bf16),
            pltpu.VMEM((2, per_step, 64, tiles * 64), bf16),
            pltpu.SemaphoreType.DMA((2, per_step)),
            pltpu.SemaphoreType.DMA((2, per_step)),
            pltpu.SemaphoreType.DMA,
        ],
        compiler_params=pltpu.CompilerParams(vmem_limit_bytes=24 << 20),
        cost_estimate=pl.CostEstimate(flops=points * 96, bytes_accessed=14 << 20, transcendentals=points),
    )(offsets, pack, below, above, pltpu.with_memory_space_constraint(coupling, pltpu.HBM))


def assemble_kernel(column_ref, own_ref, below_ref, above_ref, out_ref):
    column = column_ref[0]
    for target in range(out_ref.shape[0]):
        out_ref[target, 0:8] = own_ref[target]
        crossed = jnp.where(target < column, 0, 1)

        @pl.when(crossed == 0)
        def _():
            out_ref[target, 8:16] = below_ref[target]

        @pl.when(crossed == 1)
        def _():
            out_ref[target, 8:16] = above_ref[target]


def assemble(column, own, below, above):
    return pl.pallas_call(
        assemble_kernel,
        name="assemble",
        out_shape=jax.ShapeDtypeStruct((ROW, 16, 16, 128), bf16),
        in_specs=[SMEM] + [VMEM] * 3,
        out_specs=VMEM,
        compiler_params=pltpu.CompilerParams(vmem_limit_bytes=8 << 20),
        cost_estimate=pl.CostEstimate(flops=0, bytes_accessed=1 << 20, transcendentals=0),
    )(column, own, below, above)


def spread_matrix():
    row = lax.broadcasted_iota(jnp.int32, (128, 256), 0)
    col = lax.broadcasted_iota(jnp.int32, (128, 256), 1)
    hit = ((row // 64) == (col // 128)) & ((row % 64) == (col % 64))
    return jnp.where(hit, 1.0, 0.0).astype(bf16)


def paired(slots, pick):
    mask = low_half((16, 128))
    return jnp.concatenate([jnp.where(mask, pick(s), pick(s + 1)) for s in range(0, slots, 2)], axis=1)


def leaf_kernel(
    column_ref, leaf_refs, swapped_ref, below_ref, above_ref, one_hbm, two_hbm, out_ref, packed_ref, table_ref, sems,
):
    leaves, slots = leaf_refs.shape
    half = leaves // 2
    chunks = sems.shape[0]
    size = leaves // chunks
    copies = []
    for chunk in range(chunks):
        source, start = (one_hbm, chunk * size) if chunk * size < half else (two_hbm, chunk * size - half)
        copies.append(
            pltpu.make_async_copy(
                source.at[pl.ds(start, size)], packed_ref.at[pl.ds(chunk * size, size)], sems.at[chunk]
            )
        )
    for copy in copies:
        copy.start()
    column = column_ref[0]
    spread = spread_matrix()

    def put(window, tiles):
        out = jnp.dot(tiles.reshape(8 * 16, 128), spread, preferred_element_type=f32).astype(bf16)
        out = out.reshape(8, 16, 256)
        table_ref[pl.ds(window * 16, 8)] = out[:, :, :128]
        table_ref[pl.ds(window * 16 + 8, 8)] = out[:, :, 128:]

    put(0, below_ref[column])
    put(2 * WINDOW, above_ref[column])
    for window in range(1, 2 * WINDOW):
        place = column + window
        owner = place & (ROW - 1)
        crossed = jnp.where((place >= ROW) & (place < 2 * ROW), 0, 8)
        put(window, swapped_ref[owner, pl.ds(pl.multiple_of(crossed, 8), 8)])
    for chunk in range(chunks):
        copies[chunk].wait()
        for leaf in range(chunk * size, (chunk + 1) * size):
            out_ref[leaf] = nt(paired(slots, lambda s: table_ref[leaf_refs[leaf, s]]), packed_ref[leaf])


def leaf_local(column, leaf_refs, swapped, below, above, one, two):
    leaves, slots = leaf_refs.shape
    return pl.pallas_call(
        leaf_kernel,
        name="leaf_local",
        out_shape=jax.ShapeDtypeStruct((leaves, 16, 64), f32),
        in_specs=[SMEM] * 2 + [VMEM] * 3 + [HBM] * 2,
        out_specs=VMEM,
        scratch_shapes=[
            pltpu.VMEM((leaves,) + one.shape[1:], bf16),
            pltpu.VMEM(((2 * WINDOW + 1) * 16, 16, 128), bf16),
            pltpu.SemaphoreType.DMA((8,)),
        ],
        compiler_params=pltpu.CompilerParams(vmem_limit_bytes=16 << 20),
        cost_estimate=pl.CostEstimate(flops=140_000_000, bytes_accessed=9 << 20, transcendentals=0),
    )(column, leaf_refs, swapped, below, above, *(pltpu.with_memory_space_constraint(x, pltpu.HBM) for x in (one, two)))


def downward_kernel(
    group_refs, coarse_ref, local_ref, coupling_hbm, transfer_hbm, basis_hbm, one_hbm, two_hbm,
    out_ref, coupling_ref, transfer_ref, basis_ref, near_ref, picked_ref, sems,
):
    groups, slots = coupling_ref.shape[:2]
    half = near_ref.shape[1] // 2
    copies = [
        pltpu.make_async_copy(source, target, sems.at[i])
        for i, (source, target) in enumerate((
            (coupling_hbm, coupling_ref), (transfer_hbm, transfer_ref), (basis_hbm, basis_ref),
            (one_hbm, near_ref.at[:, :half]), (two_hbm, near_ref.at[:, half:]),
        ))
    ]
    for copy in copies:
        copy.start()
    mask = low_half((16, 128))
    for group in range(groups):
        for slot in range(slots):
            ref = group_refs[group, slot]
            tile = coarse_ref[ref >> 2, (ref >> 1) & 1]
            keep = mask == ((ref & 1) == 0)
            picked_ref[group * slots + slot] = jnp.where(keep, tile, jnp.zeros_like(tile))
    row = lax.broadcasted_iota(jnp.int32, (128, 128), 0)
    col = lax.broadcasted_iota(jnp.int32, (128, 128), 1)
    fold = jnp.where((row % 64) == (col % 64), 1.0, 0.0).astype(bf16)
    both = [
        jnp.dot(
            picked_ref[pl.ds(group * slots, slots)].reshape(slots * 16, 128), fold, preferred_element_type=f32
        ).astype(bf16).reshape(slots, 16, 128)
        for group in range(groups)
    ]
    copies[0].wait()
    local1 = [
        nt(
            paired(slots, lambda s: both[group][s]),
            jnp.concatenate([coupling_ref[group, s] for s in range(slots)], axis=1),
        ).astype(bf16)
        for group in range(groups)
    ]
    for copy in copies[1:]:
        copy.wait()
    for group in range(groups):
        leaves = range(group * 8, group * 8 + 8)
        passed = [nt(local1[group], transfer_ref[leaf]) for leaf in leaves]
        rounded = [(local_ref[leaf] + one).astype(bf16) for leaf, one in zip(leaves, passed)]
        for leaf, field in zip(leaves, rounded):
            span = slice(leaf * 128, (leaf + 1) * 128)
            out_ref[:, span] = near_ref[:, span] + jnp.dot(field, basis_ref[leaf], preferred_element_type=f32)


def downward(group_refs, coarse, local0, coupling, transfer, basis, one, two):
    groups, slots = coupling.shape[:2]
    count = one.shape[1] + two.shape[1]
    return pl.pallas_call(
        downward_kernel,
        name="downward",
        out_shape=jax.ShapeDtypeStruct((16, count), f32),
        in_specs=[SMEM] + [VMEM] * 2 + [HBM] * 5,
        out_specs=VMEM,
        scratch_shapes=[
            pltpu.VMEM(coupling.shape, bf16),
            pltpu.VMEM(transfer.shape, bf16),
            pltpu.VMEM(basis.shape, bf16),
            pltpu.VMEM((16, count), f32),
            pltpu.VMEM((groups * slots, 16, 128), bf16),
            pltpu.SemaphoreType.DMA((5,)),
        ],
        compiler_params=pltpu.CompilerParams(vmem_limit_bytes=16 << 20),
        cost_estimate=pl.CostEstimate(flops=60_000_000, bytes_accessed=5 << 20, transcendentals=0),
    )(
        group_refs, coarse, local0,
        *(pltpu.with_memory_space_constraint(x, pltpu.HBM) for x in (coupling, transfer, basis, one, two)),
    )


def shifted(shard, by, devices):
    return lax.ppermute(shard, AXES, [(i, i + by) for i in range(devices) if 0 <= i + by < devices])


def local(
    densities, points, weights, near_offsets, leaf_basis, transfer, send_lists, relay_refs, leaf_coupling,
    coarse_refs, coarse_coupling,
):
    devices = lax.axis_size(AXES)
    column = lax.rem(lax.axis_index("gy").astype(jnp.int32), ROW).reshape(1)
    rows = [[row * ROW + i for i in range(ROW)] for row in range(devices // ROW)]
    pack, rim_last, rim_first, own, up, down, coarse = upward(
        column, send_lists[0].T, densities, points, weights[None, :], leaf_basis, transfer, devices
    )
    lists_below = shifted(up, ROW, devices)
    lists_above = shifted(down, -ROW, devices)
    from_below = shifted(rim_last, 1, devices)
    from_above = shifted(rim_first, -1, devices)
    payload, from_below, from_above = lax.optimization_barrier(
        (assemble(column, own, lists_below, lists_above), from_below, from_above)
    )
    swapped = lax.all_to_all(payload, AXES, 0, 0, axis_index_groups=rows, tiled=True)
    offsets = near_offsets.T
    half = near_offsets.shape[0] // 2
    near_one, packed_one = near_field(offsets, pack, from_below, from_above, leaf_coupling, 0, half)
    swapped, coarse, pack, near_one, packed_one = lax.optimization_barrier(
        (swapped, coarse, pack, near_one, packed_one)
    )
    everyone = lax.all_to_all(coarse, AXES, 0, 0, tiled=True)
    near_two, packed_two = near_field(offsets, pack, from_below, from_above, leaf_coupling, half, half)
    local0 = leaf_local(column, relay_refs, swapped, lists_below, lists_above, packed_one, packed_two)
    return downward(
        coarse_refs, everyone, local0, coarse_coupling, transfer, leaf_basis, near_one, near_two
    )


def solution(mesh):
    in_specs = (
        P(None, AXES),
        P(None, AXES),
        P(AXES),
        P(AXES, None),
        P(AXES, None, None),
        P(AXES, None, None),
        P(AXES, None, None),
        P(AXES, None),
        P(AXES, None, None, None),
        P(AXES, None),
        P(AXES, None, None, None),
    )
    return jax.shard_map(local, mesh=mesh, in_specs=in_specs, out_specs=P(None, AXES), check_vma=False)
```

```python
import functools
import math

import jax
import jax.numpy as jnp
from jax import lax
from jax.experimental import pallas as pl
from jax.experimental.pallas import tpu as pltpu
from jax.sharding import PartitionSpec as P

AXES = ("gx", "gy")
REACH = 8
WINDOW = 8
DEPTH = 2
ROW = 8
core_square = 0.0004
four_pi = 4.0 * math.pi
f32 = jnp.float32
bf16 = jnp.bfloat16

SMEM = pl.BlockSpec(memory_space=pltpu.SMEM)
HBM = pl.BlockSpec(memory_space=pltpu.HBM)
VMEM = pl.BlockSpec(memory_space=pltpu.VMEM)


def pinned(x):
    return pltpu.with_memory_space_constraint(x, pltpu.HBM)


def kept(x):
    return pltpu.with_memory_space_constraint(x, pltpu.VMEM)


def nt(a, b):
    return lax.dot_general(a, b, (((1,), (1,)), ((), ())), preferred_element_type=f32)


def low_half(shape):
    return lax.broadcasted_iota(jnp.int32, shape, len(shape) - 1) < 64


def pieces(x):
    first = x.astype(bf16)
    rest = x - first.astype(f32)
    second = rest.astype(bf16)
    third = (rest - second.astype(f32)).astype(bf16)
    return first, second, third


def upward_kernel(
    column_ref, lists_hbm, dens_hbm, points_hbm, weights_hbm, basis_hbm, transfer_hbm,
    pack_ref, below_ref, above_ref, own_ref, up_ref, down_ref, coarse_ref,
    lists_ref, dens_ref, points_ref, weights_ref, basis_ref, transfer_ref, both_ref, sems,
):
    copies = [
        pltpu.make_async_copy(source, target, sems.at[i])
        for i, (source, target) in enumerate((
            (dens_hbm, dens_ref), (points_hbm, points_ref), (weights_hbm, weights_ref),
            (basis_hbm, basis_ref), (transfer_hbm, transfer_ref), (lists_hbm, lists_ref),
        ))
    ]
    for copy in copies:
        copy.start()
    for copy in copies[:3]:
        copy.wait()
    leaves = basis_ref.shape[0]
    rim = REACH * 128
    for part in range(4):
        span = pl.ds(part * 1024, 1024)
        scaled = dens_ref[:, span].astype(f32) * (weights_ref[:, span] * (1.0 / four_pi))
        pack_ref[0:16, span] = scaled.astype(bf16)
        one, two, three = pieces(points_ref[:, span])
        rows = jnp.concatenate(
            [one.astype(f32), two.astype(f32), three.astype(f32), jnp.zeros((7, 1024), f32)], axis=0
        )
        pack_ref[16:32, span] = rows.astype(bf16)
    below_ref[...] = pack_ref[:, -rim:]
    above_ref[...] = pack_ref[:, :rim]

    for copy in copies[3:]:
        copy.wait()
    coarse = []
    for group in range(leaves // 8):
        members = range(group * 8, group * 8 + 8)
        twice = [
            nt(dens_ref[:, leaf * 128 : (leaf + 1) * 128], jnp.concatenate([basis_ref[leaf]] * 2, axis=0)).astype(bf16)
            for leaf in members
        ]
        total = jnp.zeros((16, 64), f32)
        for leaf, rounded in zip(members, twice):
            both_ref[leaf] = rounded
            total += jnp.dot(rounded[:, :64], transfer_ref[leaf], preferred_element_type=f32)
        coarse.append(total)
    for pair in range(len(coarse) // 2):
        tile = jnp.concatenate([coarse[2 * pair], coarse[2 * pair + 1]], axis=1).astype(bf16)
        coarse_ref[:, pair] = jnp.broadcast_to(tile[None], (coarse_ref.shape[0], 16, 128))

    column = column_ref[0]
    mask = low_half((16, 128))

    def fill(target, carry):
        for ref, window in (
            (own_ref, target - column + WINDOW),
            (up_ref, jnp.minimum(target - column + 2 * WINDOW, 2 * WINDOW)),
            (down_ref, jnp.maximum(target - column, 0)),
        ):
            for slot in range(8):
                ref[target, slot] = jnp.where(
                    mask, both_ref[lists_ref[slot, window]], both_ref[lists_ref[slot + 8, window]]
                )
        return carry

    lax.fori_loop(0, ROW, fill, 0)


def upward(column, lists, densities, points, weights, basis, transfer, row_count):
    count = densities.shape[1]
    leaves = basis.shape[0]
    block = jax.ShapeDtypeStruct((ROW, 8, 16, 128), bf16)
    return pl.pallas_call(
        upward_kernel,
        name="upward",
        out_shape=(
            jax.ShapeDtypeStruct((32, count), bf16),
            jax.ShapeDtypeStruct((32, REACH * 128), bf16),
            jax.ShapeDtypeStruct((32, REACH * 128), bf16),
            block, block, block,
            jax.ShapeDtypeStruct((row_count, leaves // 16, 16, 128), bf16),
        ),
        in_specs=[SMEM] + [HBM] * 6,
        out_specs=[VMEM] * 7,
        scratch_shapes=[
            pltpu.SMEM(lists.shape, jnp.int32),
            pltpu.VMEM(densities.shape, bf16),
            pltpu.VMEM(points.shape, f32),
            pltpu.VMEM(weights.shape, f32),
            pltpu.VMEM(basis.shape, bf16),
            pltpu.VMEM(transfer.shape, bf16),
            pltpu.VMEM((leaves, 16, 128), bf16),
            pltpu.SemaphoreType.DMA((6,)),
        ],
        compiler_params=pltpu.CompilerParams(vmem_limit_bytes=12 << 20),
        cost_estimate=pl.CostEstimate(flops=20_000_000, bytes_accessed=4 << 20, transcendentals=0),
    )(column, *(pinned(x) for x in (lists, densities, points, weights, basis, transfer)))


def near_kernel(
    offsets_hbm, pack_ref, below_ref, above_ref, coupling_hbm, coarse_hbm,
    near_hbm, packed_hbm, packed_coarse_ref,
    offsets_ref, near_ref, left_ref, right_ref, wide_ref, buffer_ref, packed_ref, coarse_ref,
    sems, out_sems, more_sems,
):
    rim = REACH * 128
    inner = pack_ref.shape[1]
    leaves, tiles = coupling_hbm.shape[:2]
    per_step = buffer_ref.shape[1]
    steps = leaves // per_step

    def fetch(step, slot):
        return [
            pltpu.make_async_copy(coupling_hbm.at[step * per_step + i], buffer_ref.at[slot, i], sems.at[slot, i])
            for i in range(per_step)
        ]

    def flush(step, slot):
        return [
            pltpu.make_async_copy(packed_ref.at[slot, i], packed_hbm.at[step * per_step + i], out_sems.at[slot, i])
            for i in range(per_step)
        ]

    table = pltpu.make_async_copy(offsets_hbm, offsets_ref, more_sems.at[0])
    upper = pltpu.make_async_copy(coarse_hbm, coarse_ref, more_sems.at[1])
    table.start()
    for copy in fetch(0, 0):
        copy.start()
    upper.start()

    def merged(source, tile):
        return jnp.concatenate([source[tile], source[tile + 1]], axis=1)

    def build(source, at, start, width, own):
        wide_ref[:, pl.ds(at, width)] = source[0:16, pl.ds(start, width)]
        rows = source[16:32, pl.ds(start, width)].astype(f32)
        one, two, three = rows[0:3], rows[3:6], rows[6:9]
        whole = (one + two) + three
        square = whole[0:1] * whole[0:1] + whole[1:2] * whole[1:2] + whole[2:3] * whole[2:3]
        ones = jnp.ones((3, width), f32)
        m1, m2, m3 = (p.astype(f32) for p in pieces(square))
        fill = jnp.zeros((8, width), f32)
        right = jnp.concatenate([one, two, one, two, three, one, ones, m1, m2, m3, fill], axis=0)
        right_ref[:, pl.ds(at, width)] = right.astype(bf16)
        if own:
            n1, n2, n3 = (p.astype(f32) for p in pieces(square + core_square))
            left = jnp.concatenate(
                [-2 * one, -2 * one, -2 * two, -2 * two, -2 * one, -2 * three, n1, n2, n3, ones, fill], axis=0
            )
            left_ref[:, pl.ds(start, width)] = left.astype(bf16)

    for part in range(rim // 512):
        build(below_ref, part * 512, part * 512, 512, False)
        build(above_ref, rim + inner + part * 512, part * 512, 512, False)
    for part in range(inner // 512):
        build(pack_ref, rim + part * 512, part * 512, 512, True)

    table.wait()
    slots = offsets_ref.shape[0]

    def squares(leaf, slot):
        own = left_ref[:, pl.ds(pl.multiple_of(leaf * 128, 128), 128)]
        spans = [
            pl.ds(pl.multiple_of((leaf + REACH + offsets_ref[s, leaf]) * 128, 128), 128)
            for s in range(slot, min(slot + 2, slots))
        ]
        right = jnp.concatenate([right_ref[:, span] for span in spans], axis=1)
        wide = jnp.concatenate([wide_ref[:, span] for span in spans], axis=1)
        return wide, lax.dot_general(own, right, (((0,), (0,)), ((), ())), preferred_element_type=f32)

    def one_step(step, carry):
        slot = lax.rem(step, 2)
        for copy in fetch(step, slot):
            copy.wait()

        @pl.when(step + 1 < steps)
        def _():
            for copy in fetch(step + 1, 1 - slot):
                copy.start()

        @pl.when(step >= 2)
        def _():
            for copy in flush(step - 2, slot):
                copy.wait()

        work = [(inside, s) for inside in range(per_step) for s in range(0, slots, 2)]
        totals = [jnp.zeros((16, 128), f32)] * per_step
        ahead = [squares(step * per_step + inside, s) for inside, s in work[:DEPTH]]
        for at, (inside, s) in enumerate(work):
            leaf = step * per_step + inside
            if at + DEPTH < len(work):
                later, other = work[at + DEPTH]
                ahead.append(squares(step * per_step + later, other))
            wide, square = ahead.pop(0)
            totals[inside] += nt(wide, lax.rsqrt(square).astype(bf16))
            for tile in range(s * 2, min(s * 2 + 4, tiles) if s + 2 < slots else tiles, 2):
                packed_ref[slot, inside, :, tile * 64 : (tile + 2) * 64] = merged(buffer_ref.at[slot, inside], tile)
            if s + 2 >= slots:
                near_ref[:, pl.ds(pl.multiple_of(leaf * 128, 128), 128)] = totals[inside]
                flush(step, slot)[inside].start()
        return carry

    lax.fori_loop(0, steps, one_step, 0)
    last = pltpu.make_async_copy(near_ref, near_hbm, more_sems.at[2])
    last.start()
    upper.wait()
    for group in range(coarse_ref.shape[0]):
        for tile in range(0, tiles, 2):
            packed_coarse_ref[group, :, tile * 64 : (tile + 2) * 64] = merged(coarse_ref.at[group], tile)
    for step in range(steps - 2, steps):
        for copy in flush(step, step % 2):
            copy.wait()
    last.wait()


def near_field(offsets, pack, below, above, coupling, coarse_coupling):
    count = pack.shape[1]
    wide = count + 2 * REACH * 128
    leaves, tiles = coupling.shape[:2]
    groups = coarse_coupling.shape[0]
    per_step = 4
    points = count * offsets.shape[0] * 128
    return pl.pallas_call(
        near_kernel,
        name="near",
        out_shape=(
            pltpu.HBM((16, count), f32),
            pltpu.HBM((leaves, 64, tiles * 64), bf16),
            pltpu.VMEM((groups, 64, tiles * 64), bf16),
        ),
        in_specs=[HBM, VMEM, VMEM, VMEM, HBM, HBM],
        out_specs=[HBM, HBM, VMEM],
        scratch_shapes=[
            pltpu.SMEM(offsets.shape, jnp.int32),
            pltpu.VMEM((16, count), f32),
            pltpu.VMEM((32, count), bf16),
            pltpu.VMEM((32, wide), bf16),
            pltpu.VMEM((16, wide), bf16),
            pltpu.VMEM((2, per_step) + coupling.shape[1:], bf16),
            pltpu.VMEM((2, per_step, 64, tiles * 64), bf16),
            pltpu.VMEM(coarse_coupling.shape, bf16),
            pltpu.SemaphoreType.DMA((2, per_step)),
            pltpu.SemaphoreType.DMA((2, per_step)),
            pltpu.SemaphoreType.DMA((3,)),
        ],
        compiler_params=pltpu.CompilerParams(vmem_limit_bytes=16 << 20),
        cost_estimate=pl.CostEstimate(flops=points * 96, bytes_accessed=20 << 20, transcendentals=points),
    )(pinned(offsets), pack, below, above, pinned(coupling), pinned(coarse_coupling))


def assemble_kernel(column_ref, own_ref, below_ref, above_ref, coarse_ref, out_ref):
    column = column_ref[0]
    rows, pairs = coarse_ref.shape[:2]
    for target in range(out_ref.shape[0]):
        out_ref[target, 0:8] = own_ref[target]
        crossed = jnp.where(target < column, 0, 1)

        @pl.when(crossed == 0)
        def _():
            out_ref[target, 8:16] = below_ref[target]

        @pl.when(crossed == 1)
        def _():
            out_ref[target, 8:16] = above_ref[target]

        out_ref[target, 16:] = coarse_ref[...].reshape(rows * pairs, 16, 128)


def assemble(column, own, below, above, coarse):
    rows, pairs = coarse.shape[:2]
    return pl.pallas_call(
        assemble_kernel,
        name="assemble",
        out_shape=jax.ShapeDtypeStruct((ROW, 16 + rows * pairs, 16, 128), bf16),
        in_specs=[SMEM] + [VMEM] * 4,
        out_specs=VMEM,
        compiler_params=pltpu.CompilerParams(vmem_limit_bytes=8 << 20),
        cost_estimate=pl.CostEstimate(flops=0, bytes_accessed=3 << 20, transcendentals=0),
    )(column, own, below, above, coarse)


def spread_matrix():
    row = lax.broadcasted_iota(jnp.int32, (128, 256), 0)
    col = lax.broadcasted_iota(jnp.int32, (128, 256), 1)
    hit = ((row // 64) == (col // 128)) & ((row % 64) == (col % 64))
    return jnp.where(hit, 1.0, 0.0).astype(bf16)


def paired(slots, pick):
    mask = low_half((16, 128))
    return jnp.concatenate([jnp.where(mask, pick(s), pick(s + 1)) for s in range(0, slots, 2)], axis=1)


def finish_kernel(
    column_ref, leaf_hbm, group_hbm, swapped_ref, below_ref, above_ref, coupling_ref,
    packed_hbm, transfer_hbm, basis_hbm, near_hbm,
    out_ref, leaf_refs, group_refs, packed_ref, near_ref, transfer_ref, basis_ref, table_ref, picked_ref, sems,
):
    groups = coupling_ref.shape[0]
    slots = coupling_ref.shape[2] // 64
    copies = [
        pltpu.make_async_copy(source, target, sems.at[i])
        for i, (source, target) in enumerate((
            (group_hbm, group_refs), (leaf_hbm, leaf_refs), (transfer_hbm, transfer_ref), (basis_hbm, basis_ref),
            (near_hbm, near_ref),
        ))
    ]
    chunks = [
        pltpu.make_async_copy(packed_hbm.at[pl.ds(i * 4, 4)], packed_ref.at[pl.ds(i * 4, 4)], sems.at[5 + i])
        for i in range(2 * groups)
    ]
    copies[2:2] = chunks
    for copy in copies:
        copy.start()
    mask = low_half((16, 128))
    column = column_ref[0]
    spread = spread_matrix()

    def put(window, tiles):
        out = jnp.dot(tiles.reshape(8 * 16, 128), spread, preferred_element_type=f32).astype(bf16)
        out = out.reshape(8, 16, 256)
        table_ref[pl.ds(window * 16, 8)] = out[:, :, :128]
        table_ref[pl.ds(window * 16 + 8, 8)] = out[:, :, 128:]

    put(0, below_ref[column])
    put(2 * WINDOW, above_ref[column])
    for window in range(1, 2 * WINDOW):
        place = column + window
        owner = place & (ROW - 1)
        crossed = jnp.where((place >= ROW) & (place < 2 * ROW), 0, 8)
        put(window, swapped_ref[owner, pl.ds(pl.multiple_of(crossed, 8), 8)])

    copies[0].wait()
    for group in range(groups):
        for slot in range(slots):
            ref = group_refs[group, slot]
            tile = swapped_ref[(ref >> 2) & (ROW - 1), 16 + ((ref >> 5) << 1) + ((ref >> 1) & 1)]
            keep = mask == ((ref & 1) == 0)
            picked_ref[group * slots + slot] = jnp.where(keep, tile, jnp.zeros_like(tile))
    row = lax.broadcasted_iota(jnp.int32, (128, 128), 0)
    col = lax.broadcasted_iota(jnp.int32, (128, 128), 1)
    fold = jnp.where((row % 64) == (col % 64), 1.0, 0.0).astype(bf16)
    both = [
        jnp.dot(
            picked_ref[pl.ds(group * slots, slots)].reshape(slots * 16, 128), fold, preferred_element_type=f32
        ).astype(bf16).reshape(slots, 16, 128)
        for group in range(groups)
    ]
    local1 = [
        nt(paired(slots, lambda s: both[group][s]), coupling_ref[group]).astype(bf16) for group in range(groups)
    ]
    copies[1].wait()
    for copy in copies[2 + len(chunks):]:
        copy.wait()
    for group in range(groups):
        chunks[2 * group].wait()
        chunks[2 * group + 1].wait()
        leaves = range(group * 8, group * 8 + 8)
        fields = [nt(paired(slots, lambda s: table_ref[leaf_refs[leaf, s]]), packed_ref[leaf]) for leaf in leaves]
        passed = [nt(local1[group], transfer_ref[leaf]) for leaf in leaves]
        rounded = [(one + two).astype(bf16) for one, two in zip(fields, passed)]
        for leaf, field in zip(leaves, rounded):
            span = slice(leaf * 128, (leaf + 1) * 128)
            out_ref[:, span] = near_ref[:, span] + jnp.dot(field, basis_ref[leaf], preferred_element_type=f32)


def finish(column, leaf_refs, group_refs, swapped, below, above, packed, coupling, transfer, basis, near):
    groups = coupling.shape[0]
    slots = leaf_refs.shape[1]
    return pl.pallas_call(
        finish_kernel,
        name="finish",
        out_shape=jax.ShapeDtypeStruct(near.shape, f32),
        in_specs=[SMEM] + [HBM] * 2 + [VMEM] * 4 + [HBM] * 4,
        out_specs=VMEM,
        scratch_shapes=[
            pltpu.SMEM(leaf_refs.shape, jnp.int32),
            pltpu.SMEM(group_refs.shape, jnp.int32),
            pltpu.VMEM(packed.shape, bf16),
            pltpu.VMEM(near.shape, f32),
            pltpu.VMEM(transfer.shape, bf16),
            pltpu.VMEM(basis.shape, bf16),
            pltpu.VMEM(((2 * WINDOW + 1) * 16, 16, 128), bf16),
            pltpu.VMEM((groups * slots, 16, 128), bf16),
            pltpu.SemaphoreType.DMA((5 + 2 * groups,)),
        ],
        compiler_params=pltpu.CompilerParams(vmem_limit_bytes=20 << 20),
        cost_estimate=pl.CostEstimate(flops=200_000_000, bytes_accessed=4 << 20, transcendentals=0),
    )(
        column, pinned(leaf_refs), pinned(group_refs), swapped, below, above,
        kept(coupling), pinned(packed), pinned(transfer), pinned(basis), pinned(near),
    )


def shifted(shard, by, devices):
    return lax.ppermute(shard, AXES, [(i, i + by) for i in range(devices) if 0 <= i + by < devices])


def local(
    densities, points, weights, near_offsets, leaf_basis, transfer, send_lists, relay_refs, leaf_coupling,
    coarse_refs, coarse_coupling,
):
    devices = lax.axis_size(AXES)
    column = lax.rem(lax.axis_index("gy").astype(jnp.int32), ROW).reshape(1)
    rows = [[row * ROW + i for i in range(ROW)] for row in range(devices // ROW)]
    columns = [[col + ROW * i for i in range(devices // ROW)] for col in range(ROW)]
    pack, rim_last, rim_first, own, up, down, coarse = upward(
        column, send_lists[0].T, densities, points, weights[None, :], leaf_basis, transfer, devices // ROW
    )
    coarse_rows = lax.all_to_all(coarse, AXES, 0, 0, axis_index_groups=columns, tiled=True)
    lists_below = shifted(up, ROW, devices)
    lists_above = shifted(down, -ROW, devices)
    from_below = shifted(rim_last, 1, devices)
    from_above = shifted(rim_first, -1, devices)
    payload = assemble(column, own, lists_below, lists_above, coarse_rows)
    payload, from_below, from_above = lax.optimization_barrier((payload, from_below, from_above))
    swapped = lax.all_to_all(payload, AXES, 0, 0, axis_index_groups=rows, tiled=True)
    near, packed, packed_coarse = near_field(
        near_offsets.T, pack, from_below, from_above, leaf_coupling, coarse_coupling
    )
    return finish(
        column, relay_refs, coarse_refs, swapped, lists_below, lists_above, packed, packed_coarse, transfer,
        leaf_basis, near,
    )


def solution(mesh):
    in_specs = (
        P(None, AXES),
        P(None, AXES),
        P(AXES),
        P(AXES, None),
        P(AXES, None, None),
        P(AXES, None, None),
        P(AXES, None, None),
        P(AXES, None),
        P(AXES, None, None, None),
        P(AXES, None),
        P(AXES, None, None, None),
    )
    return jax.shard_map(local, mesh=mesh, in_specs=in_specs, out_specs=P(None, AXES), check_vma=False)
```

```python
import functools
import math

import jax
import jax.numpy as jnp
from jax import lax
from jax.experimental import pallas as pl
from jax.experimental.pallas import tpu as pltpu
from jax.sharding import PartitionSpec as P

AXES = ("gx", "gy")
REACH = 8
WINDOW = 8
DEPTH = 2
ROW = 8
core_square = 0.0004
four_pi = 4.0 * math.pi
f32 = jnp.float32
bf16 = jnp.bfloat16

SMEM = pl.BlockSpec(memory_space=pltpu.SMEM)
HBM = pl.BlockSpec(memory_space=pltpu.HBM)
VMEM = pl.BlockSpec(memory_space=pltpu.VMEM)


def pinned(x):
    return pltpu.with_memory_space_constraint(x, pltpu.HBM)


def kept(x):
    return pltpu.with_memory_space_constraint(x, pltpu.VMEM)


def nt(a, b):
    return lax.dot_general(a, b, (((1,), (1,)), ((), ())), preferred_element_type=f32)


def low_half(shape):
    return lax.broadcasted_iota(jnp.int32, shape, len(shape) - 1) < 64


def pieces(x):
    first = x.astype(bf16)
    rest = x - first.astype(f32)
    second = rest.astype(bf16)
    third = (rest - second.astype(f32)).astype(bf16)
    return first, second, third


def upward_kernel(
    column_ref, lists_hbm, dens_hbm, points_hbm, weights_hbm, basis_hbm, transfer_hbm,
    pack_ref, below_ref, above_ref, own_ref, up_ref, down_ref, coarse_ref,
    lists_ref, dens_ref, points_ref, weights_ref, basis_ref, transfer_ref, both_ref, sems,
):
    copies = [
        pltpu.make_async_copy(source, target, sems.at[i])
        for i, (source, target) in enumerate((
            (dens_hbm, dens_ref), (points_hbm, points_ref), (weights_hbm, weights_ref),
            (basis_hbm, basis_ref), (transfer_hbm, transfer_ref), (lists_hbm, lists_ref),
        ))
    ]
    for copy in copies:
        copy.start()
    for copy in copies[:3]:
        copy.wait()
    leaves = basis_ref.shape[0]
    rim = REACH * 128
    for part in range(4):
        span = pl.ds(part * 1024, 1024)
        scaled = dens_ref[:, span].astype(f32) * (weights_ref[:, span] * (1.0 / four_pi))
        pack_ref[0:16, span] = scaled.astype(bf16)
        one, two, three = pieces(points_ref[:, span])
        rows = jnp.concatenate(
            [one.astype(f32), two.astype(f32), three.astype(f32), jnp.zeros((7, 1024), f32)], axis=0
        )
        pack_ref[16:32, span] = rows.astype(bf16)
    below_ref[...] = pack_ref[:, -rim:]
    above_ref[...] = pack_ref[:, :rim]

    for copy in copies[3:]:
        copy.wait()
    coarse = []
    for group in range(leaves // 8):
        members = range(group * 8, group * 8 + 8)
        twice = [
            nt(dens_ref[:, leaf * 128 : (leaf + 1) * 128], jnp.concatenate([basis_ref[leaf]] * 2, axis=0)).astype(bf16)
            for leaf in members
        ]
        total = jnp.zeros((16, 64), f32)
        for leaf, rounded in zip(members, twice):
            both_ref[leaf] = rounded
            total += jnp.dot(rounded[:, :64], transfer_ref[leaf], preferred_element_type=f32)
        coarse.append(total)
    for pair in range(len(coarse) // 2):
        tile = jnp.concatenate([coarse[2 * pair], coarse[2 * pair + 1]], axis=1).astype(bf16)
        coarse_ref[:, pair] = jnp.broadcast_to(tile[None], (coarse_ref.shape[0], 16, 128))

    column = column_ref[0]
    mask = low_half((16, 128))

    def fill(target, carry):
        for ref, window in (
            (own_ref, target - column + WINDOW),
            (up_ref, jnp.minimum(target - column + 2 * WINDOW, 2 * WINDOW)),
            (down_ref, jnp.maximum(target - column, 0)),
        ):
            for slot in range(8):
                ref[target, slot] = jnp.where(
                    mask, both_ref[lists_ref[slot, window]], both_ref[lists_ref[slot + 8, window]]
                )
        return carry

    lax.fori_loop(0, ROW, fill, 0)


def upward(column, lists, densities, points, weights, basis, transfer, row_count):
    count = densities.shape[1]
    leaves = basis.shape[0]
    block = jax.ShapeDtypeStruct((ROW, 8, 16, 128), bf16)
    return pl.pallas_call(
        upward_kernel,
        name="upward",
        out_shape=(
            jax.ShapeDtypeStruct((32, count), bf16),
            jax.ShapeDtypeStruct((32, REACH * 128), bf16),
            jax.ShapeDtypeStruct((32, REACH * 128), bf16),
            block, block, block,
            jax.ShapeDtypeStruct((row_count, leaves // 16, 16, 128), bf16),
        ),
        in_specs=[SMEM] + [HBM] * 6,
        out_specs=[VMEM] * 7,
        scratch_shapes=[
            pltpu.SMEM(lists.shape, jnp.int32),
            pltpu.VMEM(densities.shape, bf16),
            pltpu.VMEM(points.shape, f32),
            pltpu.VMEM(weights.shape, f32),
            pltpu.VMEM(basis.shape, bf16),
            pltpu.VMEM(transfer.shape, bf16),
            pltpu.VMEM((leaves, 16, 128), bf16),
            pltpu.SemaphoreType.DMA((6,)),
        ],
        compiler_params=pltpu.CompilerParams(vmem_limit_bytes=12 << 20),
        cost_estimate=pl.CostEstimate(flops=20_000_000, bytes_accessed=4 << 20, transcendentals=0),
    )(column, *(pinned(x) for x in (lists, densities, points, weights, basis, transfer)))


def near_kernel(
    first, edge, offsets_hbm, pack_ref, below_ref, above_ref, coupling_hbm, coarse_hbm,
    near_hbm, packed_hbm, packed_coarse_ref,
    offsets_ref, near_ref, left_ref, right_ref, wide_ref, buffer_ref, packed_ref, coarse_ref,
    sems, out_sems, more_sems,
):
    rim = REACH * 128
    inner = pack_ref.shape[1]
    all_leaves, tiles = coupling_hbm.shape[:2]
    per_step = buffer_ref.shape[1]
    leaves = near_ref.shape[1] // 128
    steps = leaves // per_step

    def base(step):
        if not edge:
            return first + step * per_step
        return step * per_step + jnp.where(step < steps // 2, 0, all_leaves - leaves)

    def fetch(step, slot):
        return [
            pltpu.make_async_copy(coupling_hbm.at[base(step) + i], buffer_ref.at[slot, i], sems.at[slot, i])
            for i in range(per_step)
        ]

    def flush(step, slot):
        return [
            pltpu.make_async_copy(packed_ref.at[slot, i], packed_hbm.at[step * per_step + i], out_sems.at[slot, i])
            for i in range(per_step)
        ]

    table = pltpu.make_async_copy(offsets_hbm, offsets_ref, more_sems.at[0])
    table.start()
    for copy in fetch(0, 0):
        copy.start()
    if edge:
        upper = pltpu.make_async_copy(coarse_hbm, coarse_ref, more_sems.at[1])
        upper.start()

    def merged(source, tile):
        return jnp.concatenate([source[tile], source[tile + 1]], axis=1)

    def build(source, at, start, width, own):
        wide_ref[:, pl.ds(at, width)] = source[0:16, pl.ds(start, width)]
        rows = source[16:32, pl.ds(start, width)].astype(f32)
        one, two, three = rows[0:3], rows[3:6], rows[6:9]
        whole = (one + two) + three
        square = whole[0:1] * whole[0:1] + whole[1:2] * whole[1:2] + whole[2:3] * whole[2:3]
        ones = jnp.ones((3, width), f32)
        m1, m2, m3 = (p.astype(f32) for p in pieces(square))
        fill = jnp.zeros((8, width), f32)
        right = jnp.concatenate([one, two, one, two, three, one, ones, m1, m2, m3, fill], axis=0)
        right_ref[:, pl.ds(at, width)] = right.astype(bf16)
        if own:
            n1, n2, n3 = (p.astype(f32) for p in pieces(square + core_square))
            left = jnp.concatenate(
                [-2 * one, -2 * one, -2 * two, -2 * two, -2 * one, -2 * three, n1, n2, n3, ones, fill], axis=0
            )
            left_ref[:, pl.ds(start, width)] = left.astype(bf16)

    for part in range(rim // 512 if edge else 0):
        build(below_ref, part * 512, part * 512, 512, False)
        build(above_ref, rim + inner + part * 512, part * 512, 512, False)
    for part in range(inner // 512):
        build(pack_ref, rim + part * 512, part * 512, 512, True)

    table.wait()
    slots = offsets_ref.shape[0]

    def squares(leaf, slot):
        own = left_ref[:, pl.ds(pl.multiple_of(leaf * 128, 128), 128)]
        spans = [
            pl.ds(pl.multiple_of((leaf + REACH + offsets_ref[s, leaf]) * 128, 128), 128)
            for s in range(slot, min(slot + 2, slots))
        ]
        right = jnp.concatenate([right_ref[:, span] for span in spans], axis=1)
        wide = jnp.concatenate([wide_ref[:, span] for span in spans], axis=1)
        return wide, lax.dot_general(own, right, (((0,), (0,)), ((), ())), preferred_element_type=f32)

    def one_step(step, carry):
        slot = lax.rem(step, 2)
        for copy in fetch(step, slot):
            copy.wait()

        @pl.when(step + 1 < steps)
        def _():
            for copy in fetch(step + 1, 1 - slot):
                copy.start()

        @pl.when(step >= 2)
        def _():
            for copy in flush(step - 2, slot):
                copy.wait()

        work = [(inside, s) for inside in range(per_step) for s in range(0, slots, 2)]
        totals = [jnp.zeros((16, 128), f32)] * per_step
        ahead = [squares(base(step) + inside, s) for inside, s in work[:DEPTH]]
        for at, (inside, s) in enumerate(work):
            place = step * per_step + inside
            if at + DEPTH < len(work):
                later, other = work[at + DEPTH]
                ahead.append(squares(base(step) + later, other))
            wide, square = ahead.pop(0)
            totals[inside] += nt(wide, lax.rsqrt(square).astype(bf16))
            for tile in range(s * 2, min(s * 2 + 4, tiles) if s + 2 < slots else tiles, 2):
                packed_ref[slot, inside, :, tile * 64 : (tile + 2) * 64] = merged(buffer_ref.at[slot, inside], tile)
            if s + 2 >= slots:
                near_ref[:, pl.ds(pl.multiple_of(place * 128, 128), 128)] = totals[inside]
                pltpu.make_async_copy(packed_ref.at[slot, inside], packed_hbm.at[place], out_sems.at[slot, inside]).start()
        return carry

    lax.fori_loop(0, steps, one_step, 0)
    last = pltpu.make_async_copy(near_ref, near_hbm, more_sems.at[2])
    last.start()
    if edge:
        upper.wait()
        for group in range(coarse_ref.shape[0]):
            for tile in range(0, tiles, 2):
                packed_coarse_ref[group, :, tile * 64 : (tile + 2) * 64] = merged(coarse_ref.at[group], tile)
    for step in range(steps - 2, steps):
        for copy in flush(step, step % 2):
            copy.wait()
    last.wait()


def inner_kernel(offsets, pack, coupling, near, packed, *scratch):
    near_kernel(REACH, False, offsets, pack, None, None, coupling, None, near, packed, None, *scratch)


def edge_kernel(*refs):
    near_kernel(0, True, *refs)


def near_field(offsets, pack, rims, coupling, coarse_coupling):
    count = pack.shape[1]
    wide = count + 2 * REACH * 128
    tiles = coupling.shape[1]
    leaves = coupling.shape[0] - 2 * REACH if rims is None else 2 * REACH
    groups = coarse_coupling.shape[0]
    per_step = 4
    points = leaves * 128 * offsets.shape[0] * 128
    edge = rims is not None
    out_shape = [pltpu.HBM((16, leaves * 128), f32), pltpu.HBM((leaves, 64, tiles * 64), bf16)]
    operands = [pinned(offsets), pack] + list(rims or ()) + [pinned(coupling)]
    in_specs = [HBM] + [VMEM] * (len(operands) - 2) + [HBM]
    out_specs = [HBM, HBM]
    if edge:
        out_shape.append(pltpu.VMEM((groups, 64, tiles * 64), bf16))
        out_specs.append(VMEM)
        operands.append(pinned(coarse_coupling))
        in_specs.append(HBM)
    return pl.pallas_call(
        edge_kernel if edge else inner_kernel,
        name="near_edge" if edge else "near_inner",
        out_shape=tuple(out_shape),
        in_specs=in_specs,
        out_specs=out_specs,
        scratch_shapes=[
            pltpu.SMEM(offsets.shape, jnp.int32),
            pltpu.VMEM((16, leaves * 128), f32),
            pltpu.VMEM((32, count), bf16),
            pltpu.VMEM((32, wide), bf16),
            pltpu.VMEM((16, wide), bf16),
            pltpu.VMEM((2, per_step) + coupling.shape[1:], bf16),
            pltpu.VMEM((2, per_step, 64, tiles * 64), bf16),
            pltpu.VMEM(coarse_coupling.shape, bf16),
            pltpu.SemaphoreType.DMA((2, per_step)),
            pltpu.SemaphoreType.DMA((2, per_step)),
            pltpu.SemaphoreType.DMA((3,)),
        ],
        compiler_params=pltpu.CompilerParams(vmem_limit_bytes=16 << 20),
        cost_estimate=pl.CostEstimate(flops=points * 96, bytes_accessed=14 << 20, transcendentals=points),
    )(*operands)


def assemble_kernel(column_ref, own_ref, below_ref, above_ref, coarse_ref, out_ref):
    column = column_ref[0]
    rows, pairs = coarse_ref.shape[:2]
    for target in range(out_ref.shape[0]):
        out_ref[target, 0:8] = own_ref[target]
        crossed = jnp.where(target < column, 0, 1)

        @pl.when(crossed == 0)
        def _():
            out_ref[target, 8:16] = below_ref[target]

        @pl.when(crossed == 1)
        def _():
            out_ref[target, 8:16] = above_ref[target]

        out_ref[target, 16:] = coarse_ref[...].reshape(rows * pairs, 16, 128)


def assemble(column, own, below, above, coarse):
    rows, pairs = coarse.shape[:2]
    return pl.pallas_call(
        assemble_kernel,
        name="assemble",
        out_shape=jax.ShapeDtypeStruct((ROW, 16 + rows * pairs, 16, 128), bf16),
        in_specs=[SMEM] + [VMEM] * 4,
        out_specs=VMEM,
        compiler_params=pltpu.CompilerParams(vmem_limit_bytes=8 << 20),
        cost_estimate=pl.CostEstimate(flops=0, bytes_accessed=3 << 20, transcendentals=0),
    )(column, own, below, above, coarse)


def spread_matrix():
    row = lax.broadcasted_iota(jnp.int32, (128, 256), 0)
    col = lax.broadcasted_iota(jnp.int32, (128, 256), 1)
    hit = ((row // 64) == (col // 128)) & ((row % 64) == (col % 64))
    return jnp.where(hit, 1.0, 0.0).astype(bf16)


def paired(slots, pick):
    mask = low_half((16, 128))
    return jnp.concatenate([jnp.where(mask, pick(s), pick(s + 1)) for s in range(0, slots, 2)], axis=1)


def finish_kernel(
    column_ref, leaf_hbm, group_hbm, swapped_ref, below_ref, above_ref, coupling_ref,
    inner_hbm, edge_hbm, transfer_hbm, basis_hbm, near_inner_hbm, near_edge_hbm,
    out_ref, leaf_refs, group_refs, packed_ref, near_ref, transfer_ref, basis_ref, table_ref, picked_ref, sems,
):
    groups = coupling_ref.shape[0]
    slots = coupling_ref.shape[2] // 64
    rim = REACH * 128
    copies = [
        pltpu.make_async_copy(source, target, sems.at[i])
        for i, (source, target) in enumerate((
            (group_hbm, group_refs), (leaf_hbm, leaf_refs), (transfer_hbm, transfer_ref), (basis_hbm, basis_ref),
            (near_inner_hbm, near_ref.at[:, rim:-rim]), (near_edge_hbm.at[:, :rim], near_ref.at[:, :rim]),
            (near_edge_hbm.at[:, rim:], near_ref.at[:, -rim:]),
        ))
    ]
    chunks = []
    for i in range(2 * groups):
        if i < 2:
            source = edge_hbm.at[pl.ds(i * 4, 4)]
        elif i < 2 * groups - 2:
            source = inner_hbm.at[pl.ds(i * 4 - REACH, 4)]
        else:
            source = edge_hbm.at[pl.ds(i * 4 - 8 * groups + 2 * REACH, 4)]
        chunks.append(pltpu.make_async_copy(source, packed_ref.at[pl.ds(i * 4, 4)], sems.at[7 + i]))
    for copy in copies[:2] + chunks[:4] + copies[2:]:
        copy.start()
    mask = low_half((16, 128))
    column = column_ref[0]
    spread = spread_matrix()

    def put(window, tiles):
        out = jnp.dot(tiles.reshape(8 * 16, 128), spread, preferred_element_type=f32).astype(bf16)
        out = out.reshape(8, 16, 256)
        table_ref[pl.ds(window * 16, 8)] = out[:, :, :128]
        table_ref[pl.ds(window * 16 + 8, 8)] = out[:, :, 128:]

    put(0, below_ref[column])
    put(2 * WINDOW, above_ref[column])
    for window in range(1, 2 * WINDOW):
        place = column + window
        owner = place & (ROW - 1)
        crossed = jnp.where((place >= ROW) & (place < 2 * ROW), 0, 8)
        put(window, swapped_ref[owner, pl.ds(pl.multiple_of(crossed, 8), 8)])

    copies[0].wait()
    for group in range(groups):
        for slot in range(slots):
            ref = group_refs[group, slot]
            tile = swapped_ref[(ref >> 2) & (ROW - 1), 16 + ((ref >> 5) << 1) + ((ref >> 1) & 1)]
            keep = mask == ((ref & 1) == 0)
            picked_ref[group * slots + slot] = jnp.where(keep, tile, jnp.zeros_like(tile))
    row = lax.broadcasted_iota(jnp.int32, (128, 128), 0)
    col = lax.broadcasted_iota(jnp.int32, (128, 128), 1)
    fold = jnp.where((row % 64) == (col % 64), 1.0, 0.0).astype(bf16)
    both = [
        jnp.dot(
            picked_ref[pl.ds(group * slots, slots)].reshape(slots * 16, 128), fold, preferred_element_type=f32
        ).astype(bf16).reshape(slots, 16, 128)
        for group in range(groups)
    ]
    local1 = [
        nt(paired(slots, lambda s: both[group][s]), coupling_ref[group]).astype(bf16) for group in range(groups)
    ]
    copies[1].wait()
    for copy in copies[2:]:
        copy.wait()
    for group in range(groups):
        chunks[2 * group].wait()
        chunks[2 * group + 1].wait()
        for copy in chunks[2 * group + 4 : 2 * group + 6]:
            copy.start()
        leaves = range(group * 8, group * 8 + 8)
        fields = [nt(paired(slots, lambda s: table_ref[leaf_refs[leaf, s]]), packed_ref[leaf]) for leaf in leaves]
        passed = [nt(local1[group], transfer_ref[leaf]) for leaf in leaves]
        rounded = [(one + two).astype(bf16) for one, two in zip(fields, passed)]
        for leaf, field in zip(leaves, rounded):
            span = slice(leaf * 128, (leaf + 1) * 128)
            out_ref[:, span] = near_ref[:, span] + jnp.dot(field, basis_ref[leaf], preferred_element_type=f32)


def finish(column, leaf_refs, group_refs, swapped, below, above, inner, edge, coupling, transfer, basis, near_inner, near_edge):
    groups = coupling.shape[0]
    leaves, slots = leaf_refs.shape
    shape = (16, near_inner.shape[1] + near_edge.shape[1])
    return pl.pallas_call(
        finish_kernel,
        name="finish",
        out_shape=jax.ShapeDtypeStruct(shape, f32),
        in_specs=[SMEM] + [HBM] * 2 + [VMEM] * 4 + [HBM] * 6,
        out_specs=VMEM,
        scratch_shapes=[
            pltpu.SMEM(leaf_refs.shape, jnp.int32),
            pltpu.SMEM(group_refs.shape, jnp.int32),
            pltpu.VMEM((leaves,) + inner.shape[1:], bf16),
            pltpu.VMEM(shape, f32),
            pltpu.VMEM(transfer.shape, bf16),
            pltpu.VMEM(basis.shape, bf16),
            pltpu.VMEM(((2 * WINDOW + 1) * 16, 16, 128), bf16),
            pltpu.VMEM((groups * slots, 16, 128), bf16),
            pltpu.SemaphoreType.DMA((7 + 2 * groups,)),
        ],
        compiler_params=pltpu.CompilerParams(vmem_limit_bytes=20 << 20),
        cost_estimate=pl.CostEstimate(flops=200_000_000, bytes_accessed=4 << 20, transcendentals=0),
    )(
        column, pinned(leaf_refs), pinned(group_refs), swapped, below, above,
        kept(coupling), *(pinned(x) for x in (inner, edge, transfer, basis, near_inner, near_edge)),
    )


def shifted(shard, by, devices):
    return lax.ppermute(shard, AXES, [(i, i + by) for i in range(devices) if 0 <= i + by < devices])


def local(
    densities, points, weights, near_offsets, leaf_basis, transfer, send_lists, relay_refs, leaf_coupling,
    coarse_refs, coarse_coupling,
):
    devices = lax.axis_size(AXES)
    column = lax.rem(lax.axis_index("gy").astype(jnp.int32), ROW).reshape(1)
    rows = [[row * ROW + i for i in range(ROW)] for row in range(devices // ROW)]
    columns = [[col + ROW * i for i in range(devices // ROW)] for col in range(ROW)]
    pack, rim_last, rim_first, own, up, down, coarse = upward(
        column, send_lists[0].T, densities, points, weights[None, :], leaf_basis, transfer, devices // ROW
    )
    coarse_rows = lax.all_to_all(coarse, AXES, 0, 0, axis_index_groups=columns, tiled=True)
    lists_below = shifted(up, ROW, devices)
    lists_above = shifted(down, -ROW, devices)
    from_below = shifted(rim_last, 1, devices)
    payload = assemble(column, own, lists_below, lists_above, coarse_rows)
    payload, from_below, rim_first, pack = lax.optimization_barrier((payload, from_below, rim_first, pack))
    swapped = lax.all_to_all(payload, AXES, 0, 0, axis_index_groups=rows, tiled=True)
    rims = (from_below, shifted(rim_first, -1, devices))
    offsets = near_offsets.T
    near_inner, inner = near_field(offsets, pack, None, leaf_coupling, coarse_coupling)
    near_edge, edge, packed_coarse = near_field(offsets, pack, rims, leaf_coupling, coarse_coupling)
    return finish(
        column, relay_refs, coarse_refs, swapped, lists_below, lists_above, inner, edge, packed_coarse, transfer,
        leaf_basis, near_inner, near_edge,
    )


def solution(mesh):
    in_specs = (
        P(None, AXES),
        P(None, AXES),
        P(AXES),
        P(AXES, None),
        P(AXES, None, None),
        P(AXES, None, None),
        P(AXES, None, None),
        P(AXES, None),
        P(AXES, None, None, None),
        P(AXES, None),
        P(AXES, None, None, None),
    )
    return jax.shard_map(local, mesh=mesh, in_specs=in_specs, out_specs=P(None, AXES), check_vma=False)
```

```python
import functools
import math

import jax
import jax.numpy as jnp
from jax import lax
from jax.experimental import pallas as pl
from jax.experimental.pallas import tpu as pltpu
from jax.sharding import PartitionSpec as P

AXES = ("gx", "gy")
REACH = 8
WINDOW = 8
DEPTH = 2
ROW = 8
core_square = 0.0004
four_pi = 4.0 * math.pi
f32 = jnp.float32
bf16 = jnp.bfloat16

SMEM = pl.BlockSpec(memory_space=pltpu.SMEM)
HBM = pl.BlockSpec(memory_space=pltpu.HBM)
VMEM = pl.BlockSpec(memory_space=pltpu.VMEM)


def pinned(x):
    return pltpu.with_memory_space_constraint(x, pltpu.HBM)


def kept(x):
    return pltpu.with_memory_space_constraint(x, pltpu.VMEM)


def nt(a, b):
    return lax.dot_general(a, b, (((1,), (1,)), ((), ())), preferred_element_type=f32)


def low_half(shape):
    return lax.broadcasted_iota(jnp.int32, shape, len(shape) - 1) < 64


def pieces(x):
    first = x.astype(bf16)
    rest = x - first.astype(f32)
    second = rest.astype(bf16)
    third = (rest - second.astype(f32)).astype(bf16)
    return first, second, third


def upward_kernel(
    column_ref, lists_hbm, dens_hbm, points_hbm, weights_hbm, basis_hbm, transfer_hbm,
    pack_ref, below_ref, above_ref, own_ref, up_ref, down_ref, coarse_ref,
    lists_ref, dens_ref, points_ref, weights_ref, basis_ref, transfer_ref, both_ref, sems,
):
    copies = [
        pltpu.make_async_copy(source, target, sems.at[i])
        for i, (source, target) in enumerate((
            (dens_hbm, dens_ref), (points_hbm, points_ref), (weights_hbm, weights_ref),
            (basis_hbm, basis_ref), (transfer_hbm, transfer_ref), (lists_hbm, lists_ref),
        ))
    ]
    for copy in copies:
        copy.start()
    for copy in copies[:3]:
        copy.wait()
    leaves = basis_ref.shape[0]
    rim = REACH * 128
    for part in range(4):
        span = pl.ds(part * 1024, 1024)
        scaled = dens_ref[:, span].astype(f32) * (weights_ref[:, span] * (1.0 / four_pi))
        pack_ref[0:16, span] = scaled.astype(bf16)
        one, two, three = pieces(points_ref[:, span])
        rows = jnp.concatenate(
            [one.astype(f32), two.astype(f32), three.astype(f32), jnp.zeros((7, 1024), f32)], axis=0
        )
        pack_ref[16:32, span] = rows.astype(bf16)
    below_ref[...] = pack_ref[:, -rim:]
    above_ref[...] = pack_ref[:, :rim]

    for copy in copies[3:]:
        copy.wait()
    coarse = []
    for group in range(leaves // 8):
        members = range(group * 8, group * 8 + 8)
        twice = [
            nt(dens_ref[:, leaf * 128 : (leaf + 1) * 128], jnp.concatenate([basis_ref[leaf]] * 2, axis=0)).astype(bf16)
            for leaf in members
        ]
        total = jnp.zeros((16, 64), f32)
        for leaf, rounded in zip(members, twice):
            both_ref[leaf] = rounded
            total += jnp.dot(rounded[:, :64], transfer_ref[leaf], preferred_element_type=f32)
        coarse.append(total)
    for pair in range(len(coarse) // 2):
        tile = jnp.concatenate([coarse[2 * pair], coarse[2 * pair + 1]], axis=1).astype(bf16)
        coarse_ref[:, pair] = jnp.broadcast_to(tile[None], (coarse_ref.shape[0], 16, 128))

    column = column_ref[0]
    mask = low_half((16, 128))

    def fill(target, carry):
        for ref, window in (
            (own_ref, target - column + WINDOW),
            (up_ref, jnp.minimum(target - column + 2 * WINDOW, 2 * WINDOW)),
            (down_ref, jnp.maximum(target - column, 0)),
        ):
            for slot in range(8):
                ref[target, slot] = jnp.where(
                    mask, both_ref[lists_ref[slot, window]], both_ref[lists_ref[slot + 8, window]]
                )
        return carry

    lax.fori_loop(0, ROW, fill, 0)


def upward(column, lists, densities, points, weights, basis, transfer, row_count):
    count = densities.shape[1]
    leaves = basis.shape[0]
    block = jax.ShapeDtypeStruct((ROW, 8, 16, 128), bf16)
    return pl.pallas_call(
        upward_kernel,
        name="upward",
        out_shape=(
            jax.ShapeDtypeStruct((32, count), bf16),
            jax.ShapeDtypeStruct((32, REACH * 128), bf16),
            jax.ShapeDtypeStruct((32, REACH * 128), bf16),
            block, block, block,
            jax.ShapeDtypeStruct((row_count, leaves // 16, 16, 128), bf16),
        ),
        in_specs=[SMEM] + [HBM] * 6,
        out_specs=[VMEM] * 7,
        scratch_shapes=[
            pltpu.SMEM(lists.shape, jnp.int32),
            pltpu.VMEM(densities.shape, bf16),
            pltpu.VMEM(points.shape, f32),
            pltpu.VMEM(weights.shape, f32),
            pltpu.VMEM(basis.shape, bf16),
            pltpu.VMEM(transfer.shape, bf16),
            pltpu.VMEM((leaves, 16, 128), bf16),
            pltpu.SemaphoreType.DMA((6,)),
        ],
        compiler_params=pltpu.CompilerParams(vmem_limit_bytes=12 << 20),
        cost_estimate=pl.CostEstimate(flops=20_000_000, bytes_accessed=4 << 20, transcendentals=0),
    )(column, *(pinned(x) for x in (lists, densities, points, weights, basis, transfer)))


def near_kernel(
    first, edge, offsets_hbm, pack_ref, below_hbm, above_hbm, coupling_hbm, coarse_hbm,
    near_hbm, packed_hbm, packed_coarse_ref,
    offsets_ref, near_ref, left_ref, right_ref, wide_ref, buffer_ref, packed_ref, coarse_ref, rims_ref,
    sems, out_sems, more_sems,
):
    rim = REACH * 128
    inner = pack_ref.shape[1]
    all_leaves, tiles = coupling_hbm.shape[:2]
    per_step = buffer_ref.shape[1]
    leaves = near_ref.shape[1] // 128
    steps = leaves // per_step

    def base(step):
        if not edge:
            return first + step * per_step
        return step * per_step + jnp.where(step < steps // 2, 0, all_leaves - leaves)

    def fetch(step, slot):
        return [
            pltpu.make_async_copy(coupling_hbm.at[base(step) + i], buffer_ref.at[slot, i], sems.at[slot, i])
            for i in range(per_step)
        ]

    def flush(step, slot):
        return [
            pltpu.make_async_copy(packed_ref.at[slot, i], packed_hbm.at[step * per_step + i], out_sems.at[slot, i])
            for i in range(per_step)
        ]

    table = pltpu.make_async_copy(offsets_hbm, offsets_ref, more_sems.at[0])
    table.start()
    if edge:
        rims = [
            pltpu.make_async_copy(below_hbm, rims_ref.at[0], more_sems.at[3]),
            pltpu.make_async_copy(above_hbm, rims_ref.at[1], more_sems.at[4]),
        ]
        for copy in rims:
            copy.start()
    for copy in fetch(0, 0):
        copy.start()
    if edge:
        upper = pltpu.make_async_copy(coarse_hbm, coarse_ref, more_sems.at[1])
        upper.start()

    def merged(source, tile):
        return jnp.concatenate([source[tile], source[tile + 1]], axis=1)

    def build(source, at, start, width, own):
        wide_ref[:, pl.ds(at, width)] = source[0:16, pl.ds(start, width)]
        rows = source[16:32, pl.ds(start, width)].astype(f32)
        one, two, three = rows[0:3], rows[3:6], rows[6:9]
        whole = (one + two) + three
        square = whole[0:1] * whole[0:1] + whole[1:2] * whole[1:2] + whole[2:3] * whole[2:3]
        ones = jnp.ones((3, width), f32)
        m1, m2, m3 = (p.astype(f32) for p in pieces(square))
        fill = jnp.zeros((8, width), f32)
        right = jnp.concatenate([one, two, one, two, three, one, ones, m1, m2, m3, fill], axis=0)
        right_ref[:, pl.ds(at, width)] = right.astype(bf16)
        if own:
            n1, n2, n3 = (p.astype(f32) for p in pieces(square + core_square))
            left = jnp.concatenate(
                [-2 * one, -2 * one, -2 * two, -2 * two, -2 * one, -2 * three, n1, n2, n3, ones, fill], axis=0
            )
            left_ref[:, pl.ds(start, width)] = left.astype(bf16)

    for part in range(inner // 512):
        build(pack_ref, rim + part * 512, part * 512, 512, True)
    if edge:
        for copy in rims:
            copy.wait()
        for part in range(rim // 512):
            build(rims_ref.at[0], part * 512, part * 512, 512, False)
            build(rims_ref.at[1], rim + inner + part * 512, part * 512, 512, False)

    table.wait()
    slots = offsets_ref.shape[0]

    def squares(leaf, slot):
        own = left_ref[:, pl.ds(pl.multiple_of(leaf * 128, 128), 128)]
        spans = [
            pl.ds(pl.multiple_of((leaf + REACH + offsets_ref[s, leaf]) * 128, 128), 128)
            for s in range(slot, min(slot + 2, slots))
        ]
        right = jnp.concatenate([right_ref[:, span] for span in spans], axis=1)
        wide = jnp.concatenate([wide_ref[:, span] for span in spans], axis=1)
        return wide, lax.dot_general(own, right, (((0,), (0,)), ((), ())), preferred_element_type=f32)

    def one_step(step, carry):
        slot = lax.rem(step, 2)
        for copy in fetch(step, slot):
            copy.wait()

        @pl.when(step + 1 < steps)
        def _():
            for copy in fetch(step + 1, 1 - slot):
                copy.start()

        @pl.when(step >= 2)
        def _():
            for copy in flush(step - 2, slot):
                copy.wait()

        work = [(inside, s) for inside in range(per_step) for s in range(0, slots, 2)]
        totals = [jnp.zeros((16, 128), f32)] * per_step
        ahead = [squares(base(step) + inside, s) for inside, s in work[:DEPTH]]
        for at, (inside, s) in enumerate(work):
            place = step * per_step + inside
            if at + DEPTH < len(work):
                later, other = work[at + DEPTH]
                ahead.append(squares(base(step) + later, other))
            wide, square = ahead.pop(0)
            totals[inside] += nt(wide, lax.rsqrt(square).astype(bf16))
            for tile in range(s * 2, min(s * 2 + 4, tiles) if s + 2 < slots else tiles, 2):
                packed_ref[slot, inside, :, tile * 64 : (tile + 2) * 64] = merged(buffer_ref.at[slot, inside], tile)
            if s + 2 >= slots:
                near_ref[:, pl.ds(pl.multiple_of(place * 128, 128), 128)] = totals[inside]
                pltpu.make_async_copy(packed_ref.at[slot, inside], packed_hbm.at[place], out_sems.at[slot, inside]).start()
        return carry

    lax.fori_loop(0, steps, one_step, 0)
    last = pltpu.make_async_copy(near_ref, near_hbm, more_sems.at[2])
    last.start()
    if edge:
        upper.wait()
        for group in range(coarse_ref.shape[0]):
            for tile in range(0, tiles, 2):
                packed_coarse_ref[group, :, tile * 64 : (tile + 2) * 64] = merged(coarse_ref.at[group], tile)
    for step in range(steps - 2, steps):
        for copy in flush(step, step % 2):
            copy.wait()
    last.wait()


def inner_kernel(offsets, pack, coupling, near, packed, *scratch):
    near_kernel(REACH, False, offsets, pack, None, None, coupling, None, near, packed, None, *scratch)


def edge_kernel(*refs):
    near_kernel(0, True, *refs)


def near_field(offsets, pack, rims, coupling, coarse_coupling):
    count = pack.shape[1]
    wide = count + 2 * REACH * 128
    tiles = coupling.shape[1]
    leaves = coupling.shape[0] - 2 * REACH if rims is None else 2 * REACH
    groups = coarse_coupling.shape[0]
    per_step = 4
    points = leaves * 128 * offsets.shape[0] * 128
    edge = rims is not None
    out_shape = [pltpu.HBM((16, leaves * 128), f32), pltpu.HBM((leaves, 64, tiles * 64), bf16)]
    operands = [pinned(offsets), pack] + [pinned(x) for x in rims or ()] + [pinned(coupling)]
    in_specs = [HBM, VMEM] + [HBM] * (len(operands) - 2)
    out_specs = [HBM, HBM]
    if edge:
        out_shape.append(pltpu.VMEM((groups, 64, tiles * 64), bf16))
        out_specs.append(VMEM)
        operands.append(pinned(coarse_coupling))
        in_specs.append(HBM)
    return pl.pallas_call(
        edge_kernel if edge else inner_kernel,
        name="near_edge" if edge else "near_inner",
        out_shape=tuple(out_shape),
        in_specs=in_specs,
        out_specs=out_specs,
        scratch_shapes=[
            pltpu.SMEM(offsets.shape, jnp.int32),
            pltpu.VMEM((16, leaves * 128), f32),
            pltpu.VMEM((32, count), bf16),
            pltpu.VMEM((32, wide), bf16),
            pltpu.VMEM((16, wide), bf16),
            pltpu.VMEM((2, per_step) + coupling.shape[1:], bf16),
            pltpu.VMEM((2, per_step, 64, tiles * 64), bf16),
            pltpu.VMEM(coarse_coupling.shape, bf16),
            pltpu.VMEM((2, 32, REACH * 128), bf16),
            pltpu.SemaphoreType.DMA((2, per_step)),
            pltpu.SemaphoreType.DMA((2, per_step)),
            pltpu.SemaphoreType.DMA((5,)),
        ],
        compiler_params=pltpu.CompilerParams(vmem_limit_bytes=16 << 20),
        cost_estimate=pl.CostEstimate(flops=points * 96, bytes_accessed=14 << 20, transcendentals=points),
    )(*operands)


def assemble_kernel(column_ref, own_ref, below_ref, above_ref, coarse_ref, out_ref):
    column = column_ref[0]
    for target in range(out_ref.shape[0]):
        out_ref[target, 0:8] = own_ref[target]
        crossed = jnp.where(target < column, 0, 1)

        @pl.when(crossed == 0)
        def _():
            out_ref[target, 8:16] = below_ref[target]

        @pl.when(crossed == 1)
        def _():
            out_ref[target, 8:16] = above_ref[target]

        out_ref[target, 16:] = coarse_ref[0]


def assemble(column, own, below, above, coarse):
    return pl.pallas_call(
        assemble_kernel,
        name="assemble",
        out_shape=jax.ShapeDtypeStruct((ROW, 16 + coarse.shape[1], 16, 128), bf16),
        in_specs=[SMEM] + [VMEM] * 4,
        out_specs=VMEM,
        compiler_params=pltpu.CompilerParams(vmem_limit_bytes=4 << 20),
        cost_estimate=pl.CostEstimate(flops=0, bytes_accessed=1 << 20, transcendentals=0),
    )(column, own, below, above, coarse)


def repeat_kernel(swapped_ref, out_ref):
    pairs = out_ref.shape[2]
    for owner in range(swapped_ref.shape[0]):
        tiles = swapped_ref[owner, 16:]
        out_ref[:, owner] = jnp.broadcast_to(tiles[None], (out_ref.shape[0], pairs, 16, 128))


def repeat(swapped, rows):
    return pl.pallas_call(
        repeat_kernel,
        name="repeat",
        out_shape=jax.ShapeDtypeStruct((rows, ROW, swapped.shape[1] - 16, 16, 128), bf16),
        in_specs=[VMEM],
        out_specs=VMEM,
        compiler_params=pltpu.CompilerParams(vmem_limit_bytes=4 << 20),
        cost_estimate=pl.CostEstimate(flops=0, bytes_accessed=1 << 20, transcendentals=0),
    )(swapped)


def spread_matrix():
    row = lax.broadcasted_iota(jnp.int32, (128, 256), 0)
    col = lax.broadcasted_iota(jnp.int32, (128, 256), 1)
    hit = ((row // 64) == (col // 128)) & ((row % 64) == (col % 64))
    return jnp.where(hit, 1.0, 0.0).astype(bf16)


def paired(slots, pick):
    mask = low_half((16, 128))
    return jnp.concatenate([jnp.where(mask, pick(s), pick(s + 1)) for s in range(0, slots, 2)], axis=1)


def leaf_kernel(
    column_ref, leaf_hbm, swapped_ref, below_ref, above_ref, inner_hbm, edge_hbm,
    out_ref, leaf_refs, packed_ref, table_ref, sems,
):
    leaves, slots = leaf_refs.shape
    size = 4
    count = leaves // size
    table = pltpu.make_async_copy(leaf_hbm, leaf_refs, sems.at[count])
    table.start()
    chunks = []
    for i in range(count):
        if i * size < REACH:
            source = edge_hbm.at[pl.ds(i * size, size)]
        elif i * size < leaves - REACH:
            source = inner_hbm.at[pl.ds(i * size - REACH, size)]
        else:
            source = edge_hbm.at[pl.ds(i * size - leaves + 2 * REACH, size)]
        chunks.append(pltpu.make_async_copy(source, packed_ref.at[pl.ds(i * size, size)], sems.at[i]))
    for copy in chunks[:4]:
        copy.start()
    column = column_ref[0]
    spread = spread_matrix()

    def put(window, tiles):
        out = jnp.dot(tiles.reshape(8 * 16, 128), spread, preferred_element_type=f32).astype(bf16)
        out = out.reshape(8, 16, 256)
        table_ref[pl.ds(window * 16, 8)] = out[:, :, :128]
        table_ref[pl.ds(window * 16 + 8, 8)] = out[:, :, 128:]

    put(0, below_ref[column])
    put(2 * WINDOW, above_ref[column])
    for window in range(1, 2 * WINDOW):
        place = column + window
        owner = place & (ROW - 1)
        crossed = jnp.where((place >= ROW) & (place < 2 * ROW), 0, 8)
        put(window, swapped_ref[owner, pl.ds(pl.multiple_of(crossed, 8), 8)])
    table.wait()
    for chunk in range(count):
        chunks[chunk].wait()
        if chunk + 4 < count:
            chunks[chunk + 4].start()
        for leaf in range(chunk * size, (chunk + 1) * size):
            out_ref[leaf] = nt(paired(slots, lambda s: table_ref[leaf_refs[leaf, s]]), packed_ref[leaf])


def leaf_local(column, leaf_refs, swapped, below, above, inner, edge):
    leaves = leaf_refs.shape[0]
    return pl.pallas_call(
        leaf_kernel,
        name="leaf_local",
        out_shape=jax.ShapeDtypeStruct((leaves, 16, 64), f32),
        in_specs=[SMEM, HBM] + [VMEM] * 3 + [HBM] * 2,
        out_specs=VMEM,
        scratch_shapes=[
            pltpu.SMEM(leaf_refs.shape, jnp.int32),
            pltpu.VMEM((leaves,) + inner.shape[1:], bf16),
            pltpu.VMEM(((2 * WINDOW + 1) * 16, 16, 128), bf16),
            pltpu.SemaphoreType.DMA((leaves // 4 + 1,)),
        ],
        compiler_params=pltpu.CompilerParams(vmem_limit_bytes=16 << 20),
        cost_estimate=pl.CostEstimate(flops=140_000_000, bytes_accessed=9 << 20, transcendentals=0),
    )(column, pinned(leaf_refs), swapped, below, above, pinned(inner), pinned(edge))


def downward_kernel(
    group_hbm, coarse_ref, local_ref, coupling_ref, transfer_hbm, basis_hbm, near_inner_hbm, near_edge_hbm,
    out_ref, group_refs, transfer_ref, basis_ref, near_ref, picked_ref, sems,
):
    groups, slots = group_refs.shape
    rim = REACH * 128
    copies = [
        pltpu.make_async_copy(source, target, sems.at[i])
        for i, (source, target) in enumerate((
            (group_hbm, group_refs), (transfer_hbm, transfer_ref), (basis_hbm, basis_ref),
            (near_inner_hbm, near_ref.at[:, rim:-rim]), (near_edge_hbm.at[:, :rim], near_ref.at[:, :rim]),
            (near_edge_hbm.at[:, rim:], near_ref.at[:, -rim:]),
        ))
    ]
    for copy in copies:
        copy.start()
    mask = low_half((16, 128))
    copies[0].wait()
    for group in range(groups):
        for slot in range(slots):
            ref = group_refs[group, slot]
            tile = coarse_ref[ref >> 5, (ref >> 2) & (ROW - 1), (ref >> 1) & 1]
            keep = mask == ((ref & 1) == 0)
            picked_ref[group * slots + slot] = jnp.where(keep, tile, jnp.zeros_like(tile))
    row = lax.broadcasted_iota(jnp.int32, (128, 128), 0)
    col = lax.broadcasted_iota(jnp.int32, (128, 128), 1)
    fold = jnp.where((row % 64) == (col % 64), 1.0, 0.0).astype(bf16)
    both = [
        jnp.dot(
            picked_ref[pl.ds(group * slots, slots)].reshape(slots * 16, 128), fold, preferred_element_type=f32
        ).astype(bf16).reshape(slots, 16, 128)
        for group in range(groups)
    ]
    local1 = [
        nt(paired(slots, lambda s: both[group][s]), coupling_ref[group]).astype(bf16) for group in range(groups)
    ]
    for copy in copies[1:]:
        copy.wait()
    leaves = range(groups * 8)
    passed = [nt(local1[leaf // 8], transfer_ref[leaf]) for leaf in leaves]
    rounded = [(local_ref[leaf] + one).astype(bf16) for leaf, one in zip(leaves, passed)]
    for leaf, field in zip(leaves, rounded):
        span = slice(leaf * 128, (leaf + 1) * 128)
        out_ref[:, span] = near_ref[:, span] + jnp.dot(field, basis_ref[leaf], preferred_element_type=f32)


def downward(group_refs, coarse, local0, coupling, transfer, basis, near_inner, near_edge):
    groups, slots = group_refs.shape
    shape = (16, near_inner.shape[1] + near_edge.shape[1])
    return pl.pallas_call(
        downward_kernel,
        name="downward",
        out_shape=jax.ShapeDtypeStruct(shape, f32),
        in_specs=[HBM] + [VMEM] * 3 + [HBM] * 4,
        out_specs=VMEM,
        scratch_shapes=[
            pltpu.SMEM(group_refs.shape, jnp.int32),
            pltpu.VMEM(transfer.shape, bf16),
            pltpu.VMEM(basis.shape, bf16),
            pltpu.VMEM(shape, f32),
            pltpu.VMEM((groups * slots, 16, 128), bf16),
            pltpu.SemaphoreType.DMA((6,)),
        ],
        compiler_params=pltpu.CompilerParams(vmem_limit_bytes=8 << 20),
        cost_estimate=pl.CostEstimate(flops=60_000_000, bytes_accessed=4 << 20, transcendentals=0),
    )(
        pinned(group_refs), coarse, local0, kept(coupling),
        *(pinned(x) for x in (transfer, basis, near_inner, near_edge)),
    )


def shifted(shard, by, devices):
    return lax.ppermute(shard, AXES, [(i, i + by) for i in range(devices) if 0 <= i + by < devices])


def local(
    densities, points, weights, near_offsets, leaf_basis, transfer, send_lists, relay_refs, leaf_coupling,
    coarse_refs, coarse_coupling,
):
    devices = lax.axis_size(AXES)
    column = lax.rem(lax.axis_index("gy").astype(jnp.int32), ROW).reshape(1)
    rows = [[row * ROW + i for i in range(ROW)] for row in range(devices // ROW)]
    columns = [[col + ROW * i for i in range(devices // ROW)] for col in range(ROW)]
    pack, rim_last, rim_first, own, up, down, coarse = upward(
        column, send_lists[0].T, densities, points, weights[None, :], leaf_basis, transfer, 1
    )
    lists_below = shifted(up, ROW, devices)
    lists_above = shifted(down, -ROW, devices)
    from_below = shifted(rim_last, 1, devices)
    from_above = shifted(rim_first, -1, devices)
    payload = assemble(column, own, lists_below, lists_above, coarse)
    payload, from_below, from_above = lax.optimization_barrier((payload, from_below, from_above))
    swapped = lax.all_to_all(payload, AXES, 0, 0, axis_index_groups=rows, tiled=True)
    offsets = near_offsets.T
    near_inner, inner = near_field(offsets, pack, None, leaf_coupling, coarse_coupling)
    swapped, pack, near_inner, inner = lax.optimization_barrier((swapped, pack, near_inner, inner))
    everyone = lax.all_to_all(
        repeat(swapped, devices // ROW), AXES, 0, 0, axis_index_groups=columns, tiled=True
    )
    near_edge, edge, packed_coarse = near_field(
        offsets, pack, (from_below, from_above), leaf_coupling, coarse_coupling
    )
    local0 = leaf_local(column, relay_refs, swapped, lists_below, lists_above, inner, edge)
    return downward(
        coarse_refs, everyone, local0, packed_coarse, transfer, leaf_basis, near_inner, near_edge
    )


def solution(mesh):
    in_specs = (
        P(None, AXES),
        P(None, AXES),
        P(AXES),
        P(AXES, None),
        P(AXES, None, None),
        P(AXES, None, None),
        P(AXES, None, None),
        P(AXES, None),
        P(AXES, None, None, None),
        P(AXES, None),
        P(AXES, None, None, None),
    )
    return jax.shard_map(local, mesh=mesh, in_specs=in_specs, out_specs=P(None, AXES), check_vma=False)
```

```python
import functools
import math

import jax
import jax.numpy as jnp
from jax import lax
from jax.experimental import pallas as pl
from jax.experimental.pallas import tpu as pltpu
from jax.sharding import PartitionSpec as P

AXES = ("gx", "gy")
REACH = 8
WINDOW = 8
DEPTH = 2
ROW = 8
core_square = 0.0004
four_pi = 4.0 * math.pi
f32 = jnp.float32
bf16 = jnp.bfloat16

SMEM = pl.BlockSpec(memory_space=pltpu.SMEM)
HBM = pl.BlockSpec(memory_space=pltpu.HBM)
VMEM = pl.BlockSpec(memory_space=pltpu.VMEM)


def pinned(x):
    return pltpu.with_memory_space_constraint(x, pltpu.HBM)


def kept(x):
    return pltpu.with_memory_space_constraint(x, pltpu.VMEM)


def nt(a, b):
    return lax.dot_general(a, b, (((1,), (1,)), ((), ())), preferred_element_type=f32)


def low_half(shape):
    return lax.broadcasted_iota(jnp.int32, shape, len(shape) - 1) < 64


def pieces(x):
    first = x.astype(bf16)
    rest = x - first.astype(f32)
    second = rest.astype(bf16)
    third = (rest - second.astype(f32)).astype(bf16)
    return first, second, third


def upward_kernel(
    column_ref, lists_hbm, dens_hbm, points_hbm, weights_hbm, basis_hbm, transfer_hbm,
    pack_ref, below_ref, above_ref, own_ref, up_ref, down_ref, coarse_ref,
    lists_ref, dens_ref, points_ref, weights_ref, basis_ref, transfer_ref, both_ref, sems,
):
    copies = [
        pltpu.make_async_copy(source, target, sems.at[i])
        for i, (source, target) in enumerate((
            (dens_hbm, dens_ref), (points_hbm, points_ref), (weights_hbm, weights_ref),
            (basis_hbm, basis_ref), (transfer_hbm, transfer_ref), (lists_hbm, lists_ref),
        ))
    ]
    for copy in copies:
        copy.start()
    for copy in copies[:3]:
        copy.wait()
    leaves = basis_ref.shape[0]
    rim = REACH * 128
    for part in range(4):
        span = pl.ds(part * 1024, 1024)
        scaled = dens_ref[:, span].astype(f32) * (weights_ref[:, span] * (1.0 / four_pi))
        pack_ref[0:16, span] = scaled.astype(bf16)
        one, two, three = pieces(points_ref[:, span])
        rows = jnp.concatenate(
            [one.astype(f32), two.astype(f32), three.astype(f32), jnp.zeros((7, 1024), f32)], axis=0
        )
        pack_ref[16:32, span] = rows.astype(bf16)
    below_ref[...] = pack_ref[:, -rim:]
    above_ref[...] = pack_ref[:, :rim]

    for copy in copies[3:]:
        copy.wait()
    coarse = []
    for group in range(leaves // 8):
        members = range(group * 8, group * 8 + 8)
        twice = [
            nt(dens_ref[:, leaf * 128 : (leaf + 1) * 128], jnp.concatenate([basis_ref[leaf]] * 2, axis=0)).astype(bf16)
            for leaf in members
        ]
        total = jnp.zeros((16, 64), f32)
        for leaf, rounded in zip(members, twice):
            both_ref[leaf] = rounded
            total += jnp.dot(rounded[:, :64], transfer_ref[leaf], preferred_element_type=f32)
        coarse.append(total)
    for pair in range(len(coarse) // 2):
        tile = jnp.concatenate([coarse[2 * pair], coarse[2 * pair + 1]], axis=1).astype(bf16)
        coarse_ref[:, pair] = jnp.broadcast_to(tile[None], (coarse_ref.shape[0], 16, 128))

    column = column_ref[0]
    mask = low_half((16, 128))

    def fill(target, carry):
        for ref, window in (
            (own_ref, target - column + WINDOW),
            (up_ref, jnp.minimum(target - column + 2 * WINDOW, 2 * WINDOW)),
            (down_ref, jnp.maximum(target - column, 0)),
        ):
            for slot in range(8):
                ref[target, slot] = jnp.where(
                    mask, both_ref[lists_ref[slot, window]], both_ref[lists_ref[slot + 8, window]]
                )
        return carry

    lax.fori_loop(0, ROW, fill, 0)


def upward(column, lists, densities, points, weights, basis, transfer, row_count):
    count = densities.shape[1]
    leaves = basis.shape[0]
    block = jax.ShapeDtypeStruct((ROW, 8, 16, 128), bf16)
    return pl.pallas_call(
        upward_kernel,
        name="upward",
        out_shape=(
            jax.ShapeDtypeStruct((32, count), bf16),
            jax.ShapeDtypeStruct((32, REACH * 128), bf16),
            jax.ShapeDtypeStruct((32, REACH * 128), bf16),
            block, block, block,
            jax.ShapeDtypeStruct((row_count, leaves // 16, 16, 128), bf16),
        ),
        in_specs=[SMEM] + [HBM] * 6,
        out_specs=[VMEM] * 7,
        scratch_shapes=[
            pltpu.SMEM(lists.shape, jnp.int32),
            pltpu.VMEM(densities.shape, bf16),
            pltpu.VMEM(points.shape, f32),
            pltpu.VMEM(weights.shape, f32),
            pltpu.VMEM(basis.shape, bf16),
            pltpu.VMEM(transfer.shape, bf16),
            pltpu.VMEM((leaves, 16, 128), bf16),
            pltpu.SemaphoreType.DMA((6,)),
        ],
        compiler_params=pltpu.CompilerParams(vmem_limit_bytes=12 << 20),
        cost_estimate=pl.CostEstimate(flops=20_000_000, bytes_accessed=4 << 20, transcendentals=0),
    )(column, *(pinned(x) for x in (lists, densities, points, weights, basis, transfer)))


def near_kernel(
    offsets_hbm, pack_ref, below_ref, above_ref, coupling_hbm, coarse_hbm,
    near_hbm, packed_hbm, packed_coarse_ref,
    offsets_ref, near_ref, left_ref, right_ref, wide_ref, buffer_ref, packed_ref, coarse_ref,
    sems, out_sems, more_sems,
):
    rim = REACH * 128
    inner = pack_ref.shape[1]
    leaves, tiles = coupling_hbm.shape[:2]
    per_step = buffer_ref.shape[1]
    steps = leaves // per_step

    def fetch(step, slot):
        return [
            pltpu.make_async_copy(coupling_hbm.at[step * per_step + i], buffer_ref.at[slot, i], sems.at[slot, i])
            for i in range(per_step)
        ]

    def flush(step, slot):
        return [
            pltpu.make_async_copy(packed_ref.at[slot, i], packed_hbm.at[step * per_step + i], out_sems.at[slot, i])
            for i in range(per_step)
        ]

    table = pltpu.make_async_copy(offsets_hbm, offsets_ref, more_sems.at[0])
    upper = pltpu.make_async_copy(coarse_hbm, coarse_ref, more_sems.at[1])
    table.start()
    for copy in fetch(0, 0):
        copy.start()
    upper.start()

    def merged(source, tile):
        return jnp.concatenate([source[tile], source[tile + 1]], axis=1)

    def build(source, at, start, width, own):
        wide_ref[:, pl.ds(at, width)] = source[0:16, pl.ds(start, width)]
        rows = source[16:32, pl.ds(start, width)].astype(f32)
        one, two, three = rows[0:3], rows[3:6], rows[6:9]
        whole = (one + two) + three
        square = whole[0:1] * whole[0:1] + whole[1:2] * whole[1:2] + whole[2:3] * whole[2:3]
        ones = jnp.ones((3, width), f32)
        m1, m2, m3 = (p.astype(f32) for p in pieces(square))
        fill = jnp.zeros((8, width), f32)
        right = jnp.concatenate([one, two, one, two, three, one, ones, m1, m2, m3, fill], axis=0)
        right_ref[:, pl.ds(at, width)] = right.astype(bf16)
        if own:
            n1, n2, n3 = (p.astype(f32) for p in pieces(square + core_square))
            left = jnp.concatenate(
                [-2 * one, -2 * one, -2 * two, -2 * two, -2 * one, -2 * three, n1, n2, n3, ones, fill], axis=0
            )
            left_ref[:, pl.ds(start, width)] = left.astype(bf16)

    for part in range(rim // 512):
        build(below_ref, part * 512, part * 512, 512, False)
        build(above_ref, rim + inner + part * 512, part * 512, 512, False)
    for part in range(inner // 512):
        build(pack_ref, rim + part * 512, part * 512, 512, True)

    table.wait()
    slots = offsets_ref.shape[0]

    def squares(leaf, slot):
        own = left_ref[:, pl.ds(pl.multiple_of(leaf * 128, 128), 128)]
        spans = [
            pl.ds(pl.multiple_of((leaf + REACH + offsets_ref[s, leaf]) * 128, 128), 128)
            for s in range(slot, min(slot + 2, slots))
        ]
        right = jnp.concatenate([right_ref[:, span] for span in spans], axis=1)
        wide = jnp.concatenate([wide_ref[:, span] for span in spans], axis=1)
        return wide, lax.dot_general(own, right, (((0,), (0,)), ((), ())), preferred_element_type=f32)

    def one_step(step, carry):
        slot = lax.rem(step, 2)
        for copy in fetch(step, slot):
            copy.wait()

        @pl.when(step + 1 < steps)
        def _():
            for copy in fetch(step + 1, 1 - slot):
                copy.start()

        @pl.when(step >= 2)
        def _():
            for copy in flush(step - 2, slot):
                copy.wait()

        work = [(inside, s) for inside in range(per_step) for s in range(0, slots, 2)]
        totals = [jnp.zeros((16, 128), f32)] * per_step
        ahead = [squares(step * per_step + inside, s) for inside, s in work[:DEPTH]]
        for at, (inside, s) in enumerate(work):
            leaf = step * per_step + inside
            if at + DEPTH < len(work):
                later, other = work[at + DEPTH]
                ahead.append(squares(step * per_step + later, other))
            wide, square = ahead.pop(0)
            totals[inside] += nt(wide, lax.rsqrt(square).astype(bf16))
            for tile in range(s * 2, min(s * 2 + 4, tiles) if s + 2 < slots else tiles, 2):
                packed_ref[slot, inside, :, tile * 64 : (tile + 2) * 64] = merged(buffer_ref.at[slot, inside], tile)
            if s + 2 >= slots:
                near_ref[:, pl.ds(pl.multiple_of(leaf * 128, 128), 128)] = totals[inside]
                flush(step, slot)[inside].start()
        return carry

    lax.fori_loop(0, steps, one_step, 0)
    last = pltpu.make_async_copy(near_ref, near_hbm, more_sems.at[2])
    last.start()
    upper.wait()
    for group in range(coarse_ref.shape[0]):
        for tile in range(0, tiles, 2):
            packed_coarse_ref[group, :, tile * 64 : (tile + 2) * 64] = merged(coarse_ref.at[group], tile)
    for step in range(steps - 2, steps):
        for copy in flush(step, step % 2):
            copy.wait()
    last.wait()


def near_field(offsets, pack, below, above, coupling, coarse_coupling):
    count = pack.shape[1]
    wide = count + 2 * REACH * 128
    leaves, tiles = coupling.shape[:2]
    groups = coarse_coupling.shape[0]
    per_step = 4
    points = count * offsets.shape[0] * 128
    return pl.pallas_call(
        near_kernel,
        name="near",
        out_shape=(
            pltpu.HBM((16, count), f32),
            pltpu.HBM((leaves, 64, tiles * 64), bf16),
            pltpu.VMEM((groups, 64, tiles * 64), bf16),
        ),
        in_specs=[HBM, VMEM, VMEM, VMEM, HBM, HBM],
        out_specs=[HBM, HBM, VMEM],
        scratch_shapes=[
            pltpu.SMEM(offsets.shape, jnp.int32),
            pltpu.VMEM((16, count), f32),
            pltpu.VMEM((32, count), bf16),
            pltpu.VMEM((32, wide), bf16),
            pltpu.VMEM((16, wide), bf16),
            pltpu.VMEM((2, per_step) + coupling.shape[1:], bf16),
            pltpu.VMEM((2, per_step, 64, tiles * 64), bf16),
            pltpu.VMEM(coarse_coupling.shape, bf16),
            pltpu.SemaphoreType.DMA((2, per_step)),
            pltpu.SemaphoreType.DMA((2, per_step)),
            pltpu.SemaphoreType.DMA((3,)),
        ],
        compiler_params=pltpu.CompilerParams(vmem_limit_bytes=16 << 20),
        cost_estimate=pl.CostEstimate(flops=points * 96, bytes_accessed=20 << 20, transcendentals=points),
    )(pinned(offsets), pack, below, above, pinned(coupling), pinned(coarse_coupling))


def assemble_kernel(column_ref, own_ref, below_ref, above_ref, coarse_ref, out_ref):
    column = column_ref[0]
    rows, pairs = coarse_ref.shape[:2]
    halves = coarse_ref[...].reshape(rows // 2, 2, pairs, 16, 128)
    for target in range(out_ref.shape[0]):
        out_ref[target, 0:8] = own_ref[target]
        crossed = jnp.where(target < column, 0, 1)

        @pl.when(crossed == 0)
        def _():
            out_ref[target, 8:16] = below_ref[target]

        @pl.when(crossed == 1)
        def _():
            out_ref[target, 8:16] = above_ref[target]

        out_ref[target, 16:] = halves[:, target % 2].reshape(rows // 2 * pairs, 16, 128)


def assemble(column, own, below, above, coarse):
    rows, pairs = coarse.shape[:2]
    return pl.pallas_call(
        assemble_kernel,
        name="assemble",
        out_shape=jax.ShapeDtypeStruct((ROW, 16 + rows // 2 * pairs, 16, 128), bf16),
        in_specs=[SMEM] + [VMEM] * 4,
        out_specs=VMEM,
        compiler_params=pltpu.CompilerParams(vmem_limit_bytes=8 << 20),
        cost_estimate=pl.CostEstimate(flops=0, bytes_accessed=3 << 20, transcendentals=0),
    )(column, own, below, above, coarse)


def spread_matrix():
    row = lax.broadcasted_iota(jnp.int32, (128, 256), 0)
    col = lax.broadcasted_iota(jnp.int32, (128, 256), 1)
    hit = ((row // 64) == (col // 128)) & ((row % 64) == (col % 64))
    return jnp.where(hit, 1.0, 0.0).astype(bf16)


def paired(slots, pick):
    mask = low_half((16, 128))
    return jnp.concatenate([jnp.where(mask, pick(s), pick(s + 1)) for s in range(0, slots, 2)], axis=1)


def leaf_kernel(
    column_ref, leaf_hbm, swapped_ref, below_ref, above_ref, packed_hbm,
    out_ref, leaf_refs, packed_ref, table_ref, sems,
):
    leaves, slots = leaf_refs.shape
    size = 4
    count = leaves // size
    table = pltpu.make_async_copy(leaf_hbm, leaf_refs, sems.at[count])
    table.start()
    chunks = []
    for i in range(count):
        span = pl.ds(i * size, size)
        chunks.append(pltpu.make_async_copy(packed_hbm.at[span], packed_ref.at[span], sems.at[i]))
    for copy in chunks[:4]:
        copy.start()
    column = column_ref[0]
    spread = spread_matrix()

    def put(window, tiles):
        out = jnp.dot(tiles.reshape(8 * 16, 128), spread, preferred_element_type=f32).astype(bf16)
        out = out.reshape(8, 16, 256)
        table_ref[pl.ds(window * 16, 8)] = out[:, :, :128]
        table_ref[pl.ds(window * 16 + 8, 8)] = out[:, :, 128:]

    put(0, below_ref[column])
    put(2 * WINDOW, above_ref[column])
    for window in range(1, 2 * WINDOW):
        place = column + window
        owner = place & (ROW - 1)
        crossed = jnp.where((place >= ROW) & (place < 2 * ROW), 0, 8)
        put(window, swapped_ref[owner, pl.ds(pl.multiple_of(crossed, 8), 8)])
    table.wait()
    for chunk in range(count):
        chunks[chunk].wait()
        if chunk + 4 < count:
            chunks[chunk + 4].start()
        for leaf in range(chunk * size, (chunk + 1) * size):
            out_ref[leaf] = nt(paired(slots, lambda s: table_ref[leaf_refs[leaf, s]]), packed_ref[leaf])


def leaf_local(column, leaf_refs, swapped, below, above, packed):
    leaves = leaf_refs.shape[0]
    return pl.pallas_call(
        leaf_kernel,
        name="leaf_local",
        out_shape=jax.ShapeDtypeStruct((leaves, 16, 64), f32),
        in_specs=[SMEM, HBM] + [VMEM] * 3 + [HBM],
        out_specs=VMEM,
        scratch_shapes=[
            pltpu.SMEM(leaf_refs.shape, jnp.int32),
            pltpu.VMEM(packed.shape, bf16),
            pltpu.VMEM(((2 * WINDOW + 1) * 16, 16, 128), bf16),
            pltpu.SemaphoreType.DMA((leaves // 4 + 1,)),
        ],
        compiler_params=pltpu.CompilerParams(vmem_limit_bytes=16 << 20),
        cost_estimate=pl.CostEstimate(flops=140_000_000, bytes_accessed=9 << 20, transcendentals=0),
    )(column, pinned(leaf_refs), swapped, below, above, pinned(packed))


def downward_kernel(
    column_ref, group_hbm, swapped_ref, other_ref, local_ref, coupling_ref, transfer_hbm, basis_hbm, near_hbm,
    out_ref, group_refs, transfer_ref, basis_ref, near_ref, picked_ref, sems,
):
    groups, slots = group_refs.shape
    copies = [
        pltpu.make_async_copy(source, target, sems.at[i])
        for i, (source, target) in enumerate((
            (group_hbm, group_refs), (transfer_hbm, transfer_ref), (basis_hbm, basis_ref),
            (near_hbm, near_ref),
        ))
    ]
    for copy in copies:
        copy.start()
    mask = low_half((16, 128))
    core = column_ref[0] & 1
    copies[0].wait()
    for group in range(groups):
        for slot in range(slots):
            ref = group_refs[group, slot]
            owner = (ref >> 2) & (ROW - 1)
            place = ((ref >> 6) << 1) + ((ref >> 1) & 1)
            here = ((ref >> 5) & 1) == core
            tile = jnp.where(here, swapped_ref[owner, 16 + place], other_ref[owner, place])
            keep = mask == ((ref & 1) == 0)
            picked_ref[group * slots + slot] = jnp.where(keep, tile, jnp.zeros_like(tile))
    row = lax.broadcasted_iota(jnp.int32, (128, 128), 0)
    col = lax.broadcasted_iota(jnp.int32, (128, 128), 1)
    fold = jnp.where((row % 64) == (col % 64), 1.0, 0.0).astype(bf16)
    both = [
        jnp.dot(
            picked_ref[pl.ds(group * slots, slots)].reshape(slots * 16, 128), fold, preferred_element_type=f32
        ).astype(bf16).reshape(slots, 16, 128)
        for group in range(groups)
    ]
    local1 = [
        nt(paired(slots, lambda s: both[group][s]), coupling_ref[group]).astype(bf16) for group in range(groups)
    ]
    for copy in copies[1:]:
        copy.wait()
    leaves = range(groups * 8)
    passed = [nt(local1[leaf // 8], transfer_ref[leaf]) for leaf in leaves]
    rounded = [(local_ref[leaf] + one).astype(bf16) for leaf, one in zip(leaves, passed)]
    for leaf, field in zip(leaves, rounded):
        span = slice(leaf * 128, (leaf + 1) * 128)
        out_ref[:, span] = near_ref[:, span] + jnp.dot(field, basis_ref[leaf], preferred_element_type=f32)


def downward(column, group_refs, swapped, other, local0, coupling, transfer, basis, near):
    groups, slots = group_refs.shape
    shape = near.shape
    return pl.pallas_call(
        downward_kernel,
        name="downward",
        out_shape=jax.ShapeDtypeStruct(shape, f32),
        in_specs=[SMEM, HBM] + [VMEM] * 4 + [HBM] * 3,
        out_specs=VMEM,
        scratch_shapes=[
            pltpu.SMEM(group_refs.shape, jnp.int32),
            pltpu.VMEM(transfer.shape, bf16),
            pltpu.VMEM(basis.shape, bf16),
            pltpu.VMEM(shape, f32),
            pltpu.VMEM((groups * slots, 16, 128), bf16),
            pltpu.SemaphoreType.DMA((4,)),
        ],
        compiler_params=pltpu.CompilerParams(vmem_limit_bytes=8 << 20),
        cost_estimate=pl.CostEstimate(flops=60_000_000, bytes_accessed=4 << 20, transcendentals=0),
    )(
        column, pinned(group_refs), swapped, other, local0, kept(coupling),
        *(pinned(x) for x in (transfer, basis, near)),
    )


def shifted(shard, by, devices):
    return lax.ppermute(shard, AXES, [(i, i + by) for i in range(devices) if 0 <= i + by < devices])


def local(
    densities, points, weights, near_offsets, leaf_basis, transfer, send_lists, relay_refs, leaf_coupling,
    coarse_refs, coarse_coupling,
):
    devices = lax.axis_size(AXES)
    column = lax.rem(lax.axis_index("gy").astype(jnp.int32), ROW).reshape(1)
    rows = [[row * ROW + i for i in range(ROW)] for row in range(devices // ROW)]
    columns = [[col + ROW * i for i in range(devices // ROW)] for col in range(ROW)]
    pack, rim_last, rim_first, own, up, down, coarse = upward(
        column, send_lists[0].T, densities, points, weights[None, :], leaf_basis, transfer, devices // ROW
    )
    coarse_rows = lax.all_to_all(coarse, AXES, 0, 0, axis_index_groups=columns, tiled=True)
    lists_below = shifted(up, ROW, devices)
    lists_above = shifted(down, -ROW, devices)
    from_below = shifted(rim_last, 1, devices)
    from_above = shifted(rim_first, -1, devices)
    payload = assemble(column, own, lists_below, lists_above, coarse_rows)
    payload, from_below, from_above = lax.optimization_barrier((payload, from_below, from_above))
    swapped = lax.all_to_all(payload, AXES, 0, 0, axis_index_groups=rows, tiled=True)
    near, packed, packed_coarse = near_field(
        near_offsets.T, pack, from_below, from_above, leaf_coupling, coarse_coupling
    )
    swapped, near, packed = lax.optimization_barrier((swapped, near, packed))
    other = lax.ppermute(swapped[:, 16:], AXES, [(i, i ^ 1) for i in range(devices)])
    local0 = leaf_local(column, relay_refs, swapped, lists_below, lists_above, packed)
    return downward(
        column, coarse_refs, swapped, other, local0, packed_coarse, transfer, leaf_basis, near
    )


def solution(mesh):
    in_specs = (
        P(None, AXES),
        P(None, AXES),
        P(AXES),
        P(AXES, None),
        P(AXES, None, None),
        P(AXES, None, None),
        P(AXES, None, None),
        P(AXES, None),
        P(AXES, None, None, None),
        P(AXES, None),
        P(AXES, None, None, None),
    )
    return jax.shard_map(local, mesh=mesh, in_specs=in_specs, out_specs=P(None, AXES), check_vma=False)
```

```python
import functools
import math

import jax
import jax.numpy as jnp
from jax import lax
from jax.experimental import pallas as pl
from jax.experimental.pallas import tpu as pltpu
from jax.sharding import PartitionSpec as P

AXES = ("gx", "gy")
REACH = 8
WINDOW = 8
DEPTH = 2
ROW = 8
core_square = 0.0004
four_pi = 4.0 * math.pi
f32 = jnp.float32
bf16 = jnp.bfloat16

SMEM = pl.BlockSpec(memory_space=pltpu.SMEM)
HBM = pl.BlockSpec(memory_space=pltpu.HBM)
VMEM = pl.BlockSpec(memory_space=pltpu.VMEM)


def pinned(x):
    return pltpu.with_memory_space_constraint(x, pltpu.HBM)


def kept(x):
    return pltpu.with_memory_space_constraint(x, pltpu.VMEM)


def nt(a, b):
    return lax.dot_general(a, b, (((1,), (1,)), ((), ())), preferred_element_type=f32)


def low_half(shape):
    return lax.broadcasted_iota(jnp.int32, shape, len(shape) - 1) < 64


def pieces(x):
    first = x.astype(bf16)
    rest = x - first.astype(f32)
    second = rest.astype(bf16)
    third = (rest - second.astype(f32)).astype(bf16)
    return first, second, third


def upward_kernel(
    column_ref, lists_hbm, dens_hbm, points_hbm, weights_hbm, basis_hbm, transfer_hbm,
    pack_ref, below_ref, above_ref, own_ref, up_ref, down_ref, coarse_ref,
    lists_ref, dens_ref, points_ref, weights_ref, basis_ref, transfer_ref, both_ref, sems,
):
    copies = [
        pltpu.make_async_copy(source, target, sems.at[i])
        for i, (source, target) in enumerate((
            (dens_hbm, dens_ref), (points_hbm, points_ref), (weights_hbm, weights_ref),
            (basis_hbm, basis_ref), (transfer_hbm, transfer_ref), (lists_hbm, lists_ref),
        ))
    ]
    for copy in copies:
        copy.start()
    for copy in copies[:3]:
        copy.wait()
    leaves = basis_ref.shape[0]
    rim = REACH * 128
    for part in range(4):
        span = pl.ds(part * 1024, 1024)
        scaled = dens_ref[:, span].astype(f32) * (weights_ref[:, span] * (1.0 / four_pi))
        pack_ref[0:16, span] = scaled.astype(bf16)
        one, two, three = pieces(points_ref[:, span])
        rows = jnp.concatenate(
            [one.astype(f32), two.astype(f32), three.astype(f32), jnp.zeros((7, 1024), f32)], axis=0
        )
        pack_ref[16:32, span] = rows.astype(bf16)
    below_ref[...] = pack_ref[:, -rim:]
    above_ref[...] = pack_ref[:, :rim]

    for copy in copies[3:]:
        copy.wait()
    coarse = []
    for group in range(leaves // 8):
        members = range(group * 8, group * 8 + 8)
        twice = [
            nt(dens_ref[:, leaf * 128 : (leaf + 1) * 128], jnp.concatenate([basis_ref[leaf]] * 2, axis=0)).astype(bf16)
            for leaf in members
        ]
        total = jnp.zeros((16, 64), f32)
        for leaf, rounded in zip(members, twice):
            both_ref[leaf] = rounded
            total += jnp.dot(rounded[:, :64], transfer_ref[leaf], preferred_element_type=f32)
        coarse.append(total)
    for pair in range(len(coarse) // 2):
        tile = jnp.concatenate([coarse[2 * pair], coarse[2 * pair + 1]], axis=1).astype(bf16)
        coarse_ref[:, pair] = jnp.broadcast_to(tile[None], (coarse_ref.shape[0], 16, 128))

    column = column_ref[0]
    mask = low_half((16, 128))

    def fill(target, carry):
        for ref, window in (
            (own_ref, target - column + WINDOW),
            (up_ref, jnp.minimum(target - column + 2 * WINDOW, 2 * WINDOW)),
            (down_ref, jnp.maximum(target - column, 0)),
        ):
            for slot in range(8):
                ref[target, slot] = jnp.where(
                    mask, both_ref[lists_ref[slot, window]], both_ref[lists_ref[slot + 8, window]]
                )
        return carry

    lax.fori_loop(0, ROW, fill, 0)


def upward(column, lists, densities, points, weights, basis, transfer, row_count):
    count = densities.shape[1]
    leaves = basis.shape[0]
    block = jax.ShapeDtypeStruct((ROW, 8, 16, 128), bf16)
    return pl.pallas_call(
        upward_kernel,
        name="upward",
        out_shape=(
            jax.ShapeDtypeStruct((32, count), bf16),
            jax.ShapeDtypeStruct((32, REACH * 128), bf16),
            jax.ShapeDtypeStruct((32, REACH * 128), bf16),
            block, block, block,
            jax.ShapeDtypeStruct((row_count, leaves // 16, 16, 128), bf16),
        ),
        in_specs=[SMEM] + [HBM] * 6,
        out_specs=[VMEM] * 7,
        scratch_shapes=[
            pltpu.SMEM(lists.shape, jnp.int32),
            pltpu.VMEM(densities.shape, bf16),
            pltpu.VMEM(points.shape, f32),
            pltpu.VMEM(weights.shape, f32),
            pltpu.VMEM(basis.shape, bf16),
            pltpu.VMEM(transfer.shape, bf16),
            pltpu.VMEM((leaves, 16, 128), bf16),
            pltpu.SemaphoreType.DMA((6,)),
        ],
        compiler_params=pltpu.CompilerParams(vmem_limit_bytes=12 << 20),
        cost_estimate=pl.CostEstimate(flops=20_000_000, bytes_accessed=4 << 20, transcendentals=0),
    )(column, *(pinned(x) for x in (lists, densities, points, weights, basis, transfer)))


def near_kernel(
    offsets_hbm, pack_ref, below_ref, above_ref, coupling_hbm, coarse_hbm,
    near_hbm, packed_hbm, packed_coarse_ref,
    offsets_ref, near_ref, left_ref, right_ref, wide_ref, buffer_ref, packed_ref, coarse_ref,
    sems, out_sems, more_sems,
):
    rim = REACH * 128
    inner = pack_ref.shape[1]
    leaves, tiles = coupling_hbm.shape[:2]
    per_step = buffer_ref.shape[1]
    steps = leaves // per_step

    def fetch(step, slot):
        return [
            pltpu.make_async_copy(coupling_hbm.at[step * per_step + i], buffer_ref.at[slot, i], sems.at[slot, i])
            for i in range(per_step)
        ]

    def flush(step, slot):
        return [
            pltpu.make_async_copy(packed_ref.at[slot, i], packed_hbm.at[step * per_step + i], out_sems.at[slot, i])
            for i in range(per_step)
        ]

    table = pltpu.make_async_copy(offsets_hbm, offsets_ref, more_sems.at[0])
    upper = pltpu.make_async_copy(coarse_hbm, coarse_ref, more_sems.at[1])
    table.start()
    for copy in fetch(0, 0):
        copy.start()
    upper.start()

    def merged(source, tile):
        return jnp.concatenate([source[tile], source[tile + 1]], axis=1)

    def build(source, at, start, width, own):
        wide_ref[:, pl.ds(at, width)] = source[0:16, pl.ds(start, width)]
        rows = source[16:32, pl.ds(start, width)].astype(f32)
        one, two, three = rows[0:3], rows[3:6], rows[6:9]
        whole = (one + two) + three
        square = whole[0:1] * whole[0:1] + whole[1:2] * whole[1:2] + whole[2:3] * whole[2:3]
        ones = jnp.ones((3, width), f32)
        m1, m2, m3 = (p.astype(f32) for p in pieces(square))
        fill = jnp.zeros((8, width), f32)
        right = jnp.concatenate([one, two, one, two, three, one, ones, m1, m2, m3, fill], axis=0)
        right_ref[:, pl.ds(at, width)] = right.astype(bf16)
        if own:
            n1, n2, n3 = (p.astype(f32) for p in pieces(square + core_square))
            left = jnp.concatenate(
                [-2 * one, -2 * one, -2 * two, -2 * two, -2 * one, -2 * three, n1, n2, n3, ones, fill], axis=0
            )
            left_ref[:, pl.ds(start, width)] = left.astype(bf16)

    for part in range(rim // 512):
        build(below_ref, part * 512, part * 512, 512, False)
        build(above_ref, rim + inner + part * 512, part * 512, 512, False)
    for part in range(inner // 512):
        build(pack_ref, rim + part * 512, part * 512, 512, True)

    table.wait()
    slots = offsets_ref.shape[0]

    def squares(leaf, slot):
        own = left_ref[:, pl.ds(pl.multiple_of(leaf * 128, 128), 128)]
        spans = [
            pl.ds(pl.multiple_of((leaf + REACH + offsets_ref[s, leaf]) * 128, 128), 128)
            for s in range(slot, min(slot + 2, slots))
        ]
        right = jnp.concatenate([right_ref[:, span] for span in spans], axis=1)
        wide = jnp.concatenate([wide_ref[:, span] for span in spans], axis=1)
        return wide, lax.dot_general(own, right, (((0,), (0,)), ((), ())), preferred_element_type=f32)

    def one_step(step, carry):
        slot = lax.rem(step, 2)
        for copy in fetch(step, slot):
            copy.wait()

        @pl.when(step + 1 < steps)
        def _():
            for copy in fetch(step + 1, 1 - slot):
                copy.start()

        @pl.when(step >= 2)
        def _():
            for copy in flush(step - 2, slot):
                copy.wait()

        work = [(inside, s) for inside in range(per_step) for s in range(0, slots, 2)]
        totals = [jnp.zeros((16, 128), f32)] * per_step
        ahead = [squares(step * per_step + inside, s) for inside, s in work[:DEPTH]]
        for at, (inside, s) in enumerate(work):
            leaf = step * per_step + inside
            if at + DEPTH < len(work):
                later, other = work[at + DEPTH]
                ahead.append(squares(step * per_step + later, other))
            wide, square = ahead.pop(0)
            totals[inside] += nt(wide, lax.rsqrt(square).astype(bf16))
            for tile in range(s * 2, min(s * 2 + 4, tiles) if s + 2 < slots else tiles, 2):
                packed_ref[slot, inside, :, tile * 64 : (tile + 2) * 64] = merged(buffer_ref.at[slot, inside], tile)
            if s + 2 >= slots:
                near_ref[:, pl.ds(pl.multiple_of(leaf * 128, 128), 128)] = totals[inside]
                pltpu.make_async_copy(
                    packed_ref.at[slot, inside], packed_hbm.at[leaf], out_sems.at[slot, inside]
                ).start()
        return carry

    lax.fori_loop(0, steps, one_step, 0)
    last = pltpu.make_async_copy(near_ref, near_hbm, more_sems.at[2])
    last.start()
    upper.wait()
    for group in range(coarse_ref.shape[0]):
        for tile in range(0, tiles, 2):
            packed_coarse_ref[group, :, tile * 64 : (tile + 2) * 64] = merged(coarse_ref.at[group], tile)
    for step in range(steps - 2, steps):
        for copy in flush(step, step % 2):
            copy.wait()
    last.wait()


def near_field(offsets, pack, below, above, coupling, coarse_coupling):
    count = pack.shape[1]
    wide = count + 2 * REACH * 128
    leaves, tiles = coupling.shape[:2]
    groups = coarse_coupling.shape[0]
    per_step = 8
    points = count * offsets.shape[0] * 128
    return pl.pallas_call(
        near_kernel,
        name="near",
        out_shape=(
            pltpu.HBM((16, count), f32),
            pltpu.HBM((leaves, 64, tiles * 64), bf16),
            pltpu.VMEM((groups, 64, tiles * 64), bf16),
        ),
        in_specs=[HBM, VMEM, VMEM, VMEM, HBM, HBM],
        out_specs=[HBM, HBM, VMEM],
        scratch_shapes=[
            pltpu.SMEM(offsets.shape, jnp.int32),
            pltpu.VMEM((16, count), f32),
            pltpu.VMEM((32, count), bf16),
            pltpu.VMEM((32, wide), bf16),
            pltpu.VMEM((16, wide), bf16),
            pltpu.VMEM((2, per_step) + coupling.shape[1:], bf16),
            pltpu.VMEM((2, per_step, 64, tiles * 64), bf16),
            pltpu.VMEM(coarse_coupling.shape, bf16),
            pltpu.SemaphoreType.DMA((2, per_step)),
            pltpu.SemaphoreType.DMA((2, per_step)),
            pltpu.SemaphoreType.DMA((3,)),
        ],
        compiler_params=pltpu.CompilerParams(vmem_limit_bytes=28 << 20),
        cost_estimate=pl.CostEstimate(flops=points * 96, bytes_accessed=20 << 20, transcendentals=points),
    )(pinned(offsets), pack, below, above, pinned(coupling), pinned(coarse_coupling))


def assemble_kernel(column_ref, own_ref, below_ref, above_ref, coarse_ref, out_ref):
    column = column_ref[0]
    rows, pairs = coarse_ref.shape[:2]
    halves = coarse_ref[...].reshape(rows // 2, 2, pairs, 16, 128)
    for target in range(out_ref.shape[0]):
        out_ref[target, 0:8] = own_ref[target]
        crossed = jnp.where(target < column, 0, 1)

        @pl.when(crossed == 0)
        def _():
            out_ref[target, 8:16] = below_ref[target]

        @pl.when(crossed == 1)
        def _():
            out_ref[target, 8:16] = above_ref[target]

        out_ref[target, 16:] = halves[:, target % 2].reshape(rows // 2 * pairs, 16, 128)


def assemble(column, own, below, above, coarse):
    rows, pairs = coarse.shape[:2]
    return pl.pallas_call(
        assemble_kernel,
        name="assemble",
        out_shape=jax.ShapeDtypeStruct((ROW, 16 + rows // 2 * pairs, 16, 128), bf16),
        in_specs=[SMEM] + [VMEM] * 4,
        out_specs=VMEM,
        compiler_params=pltpu.CompilerParams(vmem_limit_bytes=8 << 20),
        cost_estimate=pl.CostEstimate(flops=0, bytes_accessed=3 << 20, transcendentals=0),
    )(column, own, below, above, coarse)


def spread_matrix():
    row = lax.broadcasted_iota(jnp.int32, (128, 256), 0)
    col = lax.broadcasted_iota(jnp.int32, (128, 256), 1)
    hit = ((row // 64) == (col // 128)) & ((row % 64) == (col % 64))
    return jnp.where(hit, 1.0, 0.0).astype(bf16)


def paired(slots, pick):
    mask = low_half((16, 128))
    return jnp.concatenate([jnp.where(mask, pick(s), pick(s + 1)) for s in range(0, slots, 2)], axis=1)


def leaf_kernel(
    column_ref, leaf_hbm, swapped_ref, below_ref, above_ref, packed_hbm,
    out_ref, leaf_refs, packed_ref, table_ref, sems,
):
    leaves, slots = leaf_refs.shape
    size = 4
    count = leaves // size
    table = pltpu.make_async_copy(leaf_hbm, leaf_refs, sems.at[count])
    table.start()
    chunks = []
    for i in range(count):
        span = pl.ds(i * size, size)
        chunks.append(pltpu.make_async_copy(packed_hbm.at[span], packed_ref.at[span], sems.at[i]))
    for copy in chunks[:4]:
        copy.start()
    column = column_ref[0]
    spread = spread_matrix()

    def put(window, tiles):
        out = jnp.dot(tiles.reshape(8 * 16, 128), spread, preferred_element_type=f32).astype(bf16)
        out = out.reshape(8, 16, 256)
        table_ref[pl.ds(window * 16, 8)] = out[:, :, :128]
        table_ref[pl.ds(window * 16 + 8, 8)] = out[:, :, 128:]

    put(0, below_ref[column])
    put(2 * WINDOW, above_ref[column])
    for window in range(1, 2 * WINDOW):
        place = column + window
        owner = place & (ROW - 1)
        crossed = jnp.where((place >= ROW) & (place < 2 * ROW), 0, 8)
        put(window, swapped_ref[owner, pl.ds(pl.multiple_of(crossed, 8), 8)])
    table.wait()
    for chunk in range(count):
        chunks[chunk].wait()
        if chunk + 4 < count:
            chunks[chunk + 4].start()
        for leaf in range(chunk * size, (chunk + 1) * size):
            out_ref[leaf] = nt(paired(slots, lambda s: table_ref[leaf_refs[leaf, s]]), packed_ref[leaf])


def leaf_local(column, leaf_refs, swapped, below, above, packed):
    leaves = leaf_refs.shape[0]
    return pl.pallas_call(
        leaf_kernel,
        name="leaf_local",
        out_shape=jax.ShapeDtypeStruct((leaves, 16, 64), f32),
        in_specs=[SMEM, HBM] + [VMEM] * 3 + [HBM],
        out_specs=VMEM,
        scratch_shapes=[
            pltpu.SMEM(leaf_refs.shape, jnp.int32),
            pltpu.VMEM(packed.shape, bf16),
            pltpu.VMEM(((2 * WINDOW + 1) * 16, 16, 128), bf16),
            pltpu.SemaphoreType.DMA((leaves // 4 + 1,)),
        ],
        compiler_params=pltpu.CompilerParams(vmem_limit_bytes=16 << 20),
        cost_estimate=pl.CostEstimate(flops=140_000_000, bytes_accessed=9 << 20, transcendentals=0),
    )(column, pinned(leaf_refs), swapped, below, above, pinned(packed))


def downward_kernel(
    column_ref, group_hbm, swapped_ref, other_ref, local_ref, coupling_ref, transfer_hbm, basis_hbm, near_hbm,
    out_ref, group_refs, transfer_ref, basis_ref, near_ref, picked_ref, sems,
):
    groups, slots = group_refs.shape
    copies = [
        pltpu.make_async_copy(source, target, sems.at[i])
        for i, (source, target) in enumerate((
            (group_hbm, group_refs), (transfer_hbm, transfer_ref), (basis_hbm, basis_ref),
            (near_hbm, near_ref),
        ))
    ]
    for copy in copies:
        copy.start()
    mask = low_half((16, 128))
    core = column_ref[0] & 1
    copies[0].wait()
    for group in range(groups):
        for slot in range(slots):
            ref = group_refs[group, slot]
            owner = (ref >> 2) & (ROW - 1)
            place = ((ref >> 6) << 1) + ((ref >> 1) & 1)
            here = ((ref >> 5) & 1) == core
            tile = jnp.where(here, swapped_ref[owner, 16 + place], other_ref[owner, place])
            keep = mask == ((ref & 1) == 0)
            picked_ref[group * slots + slot] = jnp.where(keep, tile, jnp.zeros_like(tile))
    row = lax.broadcasted_iota(jnp.int32, (128, 128), 0)
    col = lax.broadcasted_iota(jnp.int32, (128, 128), 1)
    fold = jnp.where((row % 64) == (col % 64), 1.0, 0.0).astype(bf16)
    both = [
        jnp.dot(
            picked_ref[pl.ds(group * slots, slots)].reshape(slots * 16, 128), fold, preferred_element_type=f32
        ).astype(bf16).reshape(slots, 16, 128)
        for group in range(groups)
    ]
    local1 = [
        nt(paired(slots, lambda s: both[group][s]), coupling_ref[group]).astype(bf16) for group in range(groups)
    ]
    for copy in copies[1:]:
        copy.wait()
    leaves = range(groups * 8)
    passed = [nt(local1[leaf // 8], transfer_ref[leaf]) for leaf in leaves]
    rounded = [(local_ref[leaf] + one).astype(bf16) for leaf, one in zip(leaves, passed)]
    for leaf, field in zip(leaves, rounded):
        span = slice(leaf * 128, (leaf + 1) * 128)
        out_ref[:, span] = near_ref[:, span] + jnp.dot(field, basis_ref[leaf], preferred_element_type=f32)


def downward(column, group_refs, swapped, other, local0, coupling, transfer, basis, near):
    groups, slots = group_refs.shape
    shape = near.shape
    return pl.pallas_call(
        downward_kernel,
        name="downward",
        out_shape=jax.ShapeDtypeStruct(shape, f32),
        in_specs=[SMEM, HBM] + [VMEM] * 4 + [HBM] * 3,
        out_specs=VMEM,
        scratch_shapes=[
            pltpu.SMEM(group_refs.shape, jnp.int32),
            pltpu.VMEM(transfer.shape, bf16),
            pltpu.VMEM(basis.shape, bf16),
            pltpu.VMEM(shape, f32),
            pltpu.VMEM((groups * slots, 16, 128), bf16),
            pltpu.SemaphoreType.DMA((4,)),
        ],
        compiler_params=pltpu.CompilerParams(vmem_limit_bytes=8 << 20),
        cost_estimate=pl.CostEstimate(flops=60_000_000, bytes_accessed=4 << 20, transcendentals=0),
    )(
        column, pinned(group_refs), swapped, other, local0, kept(coupling),
        *(pinned(x) for x in (transfer, basis, near)),
    )


def shifted(shard, by, devices):
    return lax.ppermute(shard, AXES, [(i, i + by) for i in range(devices) if 0 <= i + by < devices])


def local(
    densities, points, weights, near_offsets, leaf_basis, transfer, send_lists, relay_refs, leaf_coupling,
    coarse_refs, coarse_coupling,
):
    devices = lax.axis_size(AXES)
    column = lax.rem(lax.axis_index("gy").astype(jnp.int32), ROW).reshape(1)
    rows = [[row * ROW + i for i in range(ROW)] for row in range(devices // ROW)]
    columns = [[col + ROW * i for i in range(devices // ROW)] for col in range(ROW)]
    pack, rim_last, rim_first, own, up, down, coarse = upward(
        column, send_lists[0].T, densities, points, weights[None, :], leaf_basis, transfer, devices // ROW
    )
    coarse_rows = lax.all_to_all(coarse, AXES, 0, 0, axis_index_groups=columns, tiled=True)
    lists_below = shifted(up, ROW, devices)
    lists_above = shifted(down, -ROW, devices)
    from_below = shifted(rim_last, 1, devices)
    from_above = shifted(rim_first, -1, devices)
    payload = assemble(column, own, lists_below, lists_above, coarse_rows)
    payload, from_below, from_above = lax.optimization_barrier((payload, from_below, from_above))
    swapped = lax.all_to_all(payload, AXES, 0, 0, axis_index_groups=rows, tiled=True)
    near, packed, packed_coarse = near_field(
        near_offsets.T, pack, from_below, from_above, leaf_coupling, coarse_coupling
    )
    swapped, near, packed = lax.optimization_barrier((swapped, near, packed))
    other = lax.ppermute(swapped[:, 16:], AXES, [(i, i ^ 1) for i in range(devices)])
    local0 = leaf_local(column, relay_refs, swapped, lists_below, lists_above, packed)
    return downward(
        column, coarse_refs, swapped, other, local0, packed_coarse, transfer, leaf_basis, near
    )


def solution(mesh):
    in_specs = (
        P(None, AXES),
        P(None, AXES),
        P(AXES),
        P(AXES, None),
        P(AXES, None, None),
        P(AXES, None, None),
        P(AXES, None, None),
        P(AXES, None),
        P(AXES, None, None, None),
        P(AXES, None),
        P(AXES, None, None, None),
    )
    return jax.shard_map(local, mesh=mesh, in_specs=in_specs, out_specs=P(None, AXES), check_vma=False)
```
